128 devices in a mesh: sect: 2 (over core), tmpl: 64 (over z, y, x).
Axes of the slice: x: 4, y: 4, z: 4, core: 2. Of those that a mesh axis runs over, the one named last changes fastest.
Arguments:
- strain: bfloat16 [2, 1535], P('sect'), may hold values from -6 to 6
- filters: bfloat16 [2, 1024, 1024], P('sect', 'tmpl'), may hold values from -0.1875 to 0.1875
- synthesis: bfloat16 [2, 32768, 1024], P('sect', 'tmpl'), may hold values from -0.1875 to 0.1875
- correlation: float32 [16384, 2, 351], P('tmpl'), may hold values from -0.6 to 0.6
Outputs:
- snr: bfloat16 [32768, 512], P('tmpl', 'sect')
- residual: float32 [16384, 512], P('tmpl', 'sect')
The draws below stay inside these ranges and needn't reach their ends.
All inputs are finite; a program needn't handle non-finite values.
Results may differ from the reference program's by a relative error of at most 0.0049.
Values may be sent and summed in bfloat16 or wider, within the bound.
No kernel may reach another device: no remote copies, remote signals or barrier semaphores. Data moves between devices by JAX's collectives and lax.ppermute only.
A program may use at most 64 MiB of HBM per device.

```python
import jax
import jax.numpy as jnp
from jax import lax

TEMPLATES = 16384
BASES = 1024
TAPS = 1024
ACL = 351
KMAX = 4
SAMPLES = 512
SECTIONS = 2
COLUMNS = 32768
DATA_LEN = 1535


def steps_of(own_key, dims, pieces, low, largest):
    def one(dim, shards_of):
        draws = jax.random.uniform(jax.random.fold_in(jax.random.fold_in(own_key, 6), dim), (shards_of,), jnp.float32, low / len(pieces), largest / len(pieces))
        return jnp.repeat(jnp.exp(draws), dims[dim] // shards_of).reshape((-1,) + (1,) * (len(dims) - dim - 1))

    gain = one(*pieces[0])
    for cut in pieces[1:]:
        gain = gain * one(*cut)
    return gain


def scatter_about(rng, dims, deviation, most, split=(), kind=jnp.bfloat16):
    entries = jax.random.normal(rng, dims, jnp.float32) * deviation
    if len(split) > 0:
        entries = steps_of(rng, dims, split, -0.22, 0.18) * entries
    return jnp.clip(entries, min=-most, max=most).astype(kind)


def setup_inputs(seed: int = 0) -> dict:
    streams_of = jax.random.split(jax.random.key(seed), 5)
    return {
        "strain": scatter_about(streams_of[0], (SECTIONS, DATA_LEN), 1.0, 6.0, ((0, 2),)),
        "filters": scatter_about(streams_of[1], (SECTIONS, BASES, TAPS), TAPS ** -0.5, 0.1875, ((0, 2), (1, 64))),
        "synthesis": scatter_about(streams_of[2], (SECTIONS, COLUMNS, BASES), BASES ** -0.5, 0.1875, ((0, 2), (1, 64))),
        "correlation": scatter_about(streams_of[3], (TEMPLATES, 2, ACL), 0.1, 0.6, ((0, 64),), jnp.float32),
    }


def residual_terms(window, centre, correlation):
    groups = correlation.shape[0]
    length = correlation.shape[2]
    real_part = correlation[:, 0, :]
    imag_part = correlation[:, 1, :]
    first = jnp.stack([real_part, imag_part], axis=1)
    second = jnp.stack([imag_part, -real_part], axis=1)
    kernel = jnp.stack([first, second], axis=1).reshape(2 * groups, 2, length)
    products = lax.conv_general_dilated(window[None], kernel, (1,), "VALID", dimension_numbers=("NCH", "OIH", "NCH"), feature_group_count=groups, precision=lax.Precision.HIGHEST)[0]
    outlen = centre.shape[1]
    products = products.reshape(groups, 2, outlen)
    framed = window.reshape(groups, 2, window.shape[1])
    power = framed[:, 0] * framed[:, 0] + framed[:, 1] * framed[:, 1]
    energy = lax.reduce_window(power, jnp.float32(0.0), lax.add, (1, length), (1, 1), "VALID")
    middle = centre.reshape(groups, 2, outlen)
    weight = jnp.sum(real_part * real_part + imag_part * imag_part, axis=1)[:, None]
    cross = middle[:, 0] * products[:, 0] - middle[:, 1] * products[:, 1]
    magnitude = middle[:, 0] * middle[:, 0] + middle[:, 1] * middle[:, 1]
    return (energy - 2.0 * cross + magnitude * weight) / (2.0 * length)


def reference(strain, filters, synthesis, correlation):
    accum = None
    for section in range(SECTIONS):
        divisor_log = min(SECTIONS - 1 - section, KMAX)
        count = SAMPLES >> divisor_log
        signal = strain[section, : count + TAPS - 1]
        basis = lax.conv_general_dilated(signal[None, None, :], filters[section][:, None, :], (1,), "VALID", dimension_numbers=("NCH", "OIH", "NCH"), preferred_element_type=jnp.float32)[0].astype(jnp.bfloat16)
        partial_value = jnp.dot(synthesis[section], basis, preferred_element_type=jnp.float32)
        if accum is None:
            accum = partial_value
        else:
            factor = count // accum.shape[1]
            accum = jnp.repeat(accum, factor, axis=1) + partial_value
    half = (ACL - 1) // 2
    padded = jnp.pad(accum, ((0, 0), (half, half)))
    groups = min(TEMPLATES, 256)
    blocks = TEMPLATES // groups
    windows = padded.reshape(blocks, 2 * groups, padded.shape[1])
    centres = accum.reshape(blocks, 2 * groups, SAMPLES)
    series = correlation.reshape(blocks, groups, 2, ACL)
    residual = lax.map(lambda item: residual_terms(item[0], item[1], item[2]), (windows, centres, series))
    return accum.astype(jnp.bfloat16), residual.reshape(TEMPLATES, SAMPLES)
```

```python
import functools

import jax
import jax.numpy as jnp
import numpy as np
from jax import lax
from jax.experimental import pallas as pl
from jax.experimental.pallas import tpu as pltpu
from jax.sharding import PartitionSpec as P

KMAX = 4
PERIOD = 767
BINS = 384
LANES = 128


def forward_matrix(rows):
    angle = 2.0 * np.pi * np.outer(np.arange(rows), np.arange(BINS)) / PERIOD
    return np.concatenate([np.cos(angle), -np.sin(angle)], axis=1)


def inverse_matrix(samples, half):
    angle = 2.0 * np.pi * np.outer(np.arange(BINS), np.arange(samples) - half) / PERIOD
    share = np.where(np.arange(BINS) == 0, 0.5, 1.0)[:, None]
    return np.concatenate([share * np.cos(angle), -share * np.sin(angle)], axis=0)


def conv_kernel(strain_ref, filters_ref, basis_ref, line_ref):
    section = lax.axis_index("sect")
    taps = filters_ref.shape[1]
    samples = basis_ref.shape[1]
    width = line_ref.shape[1]
    rows = 256
    line_ref[...] = jnp.zeros_like(line_ref)
    line_ref[0:1, 0 : strain_ref.shape[1]] = strain_ref[...].astype(jnp.float32)
    spread = jnp.broadcast_to(line_ref[0:1, :], (rows, width))
    shifted = pltpu.roll(spread, width - (rows - 1), 1, stride=1, stride_axis=0).astype(jnp.bfloat16)
    row = lax.broadcasted_iota(jnp.int32, (rows, rows), 0)
    col = lax.broadcasted_iota(jnp.int32, (rows, rows), 1)
    flip = (row + col == rows - 1).astype(jnp.float32).astype(jnp.bfloat16)
    total = jnp.zeros((filters_ref.shape[0], samples), jnp.float32)
    for start in range(0, taps, rows):
        part = jnp.dot(filters_ref[:, start : start + rows], flip, preferred_element_type=jnp.float32)
        total += jnp.dot(
            part.astype(jnp.bfloat16), shifted[:, start : start + samples], preferred_element_type=jnp.float32
        )
    basis = total.astype(jnp.bfloat16)
    source = lax.broadcasted_iota(jnp.int32, (samples, samples), 0)
    target = lax.broadcasted_iota(jnp.int32, (samples, samples), 1)
    hold_log = lax.axis_size("sect") - 1 - section
    pick = (source == (target >> hold_log)).astype(jnp.float32).astype(jnp.bfloat16)
    basis_ref[...] = jnp.dot(basis, pick, preferred_element_type=jnp.float32).astype(jnp.bfloat16)


def held_basis(strain, filters, samples):
    width = strain.shape[1] + 1
    return pl.pallas_call(
        conv_kernel,
        out_shape=jax.ShapeDtypeStruct((filters.shape[0], samples), jnp.bfloat16),
        scratch_shapes=[pltpu.VMEM((8, width), jnp.float32)],
        name="held_basis",
    )(strain, filters)


def lags_kernel(series_ref, forward_ref, spectrum_ref, weight_ref):
    groups = weight_ref.shape[0]
    length = series_ref.shape[1]
    real_part = series_ref[0:groups, :]
    imag_part = series_ref[groups:, :]
    weight_ref[...] = jnp.sum(real_part * real_part + imag_part * imag_part, axis=1, keepdims=True)
    table = forward_ref[0:length, :]
    spectrum_ref[0:groups, :] = jnp.dot(real_part.astype(jnp.bfloat16), table, preferred_element_type=jnp.float32)
    spectrum_ref[groups:, :] = jnp.dot(imag_part.astype(jnp.bfloat16), table, preferred_element_type=jnp.float32)


def lag_spectrum(correlation, forward):
    groups, _, length = correlation.shape
    return pl.pallas_call(
        lags_kernel,
        out_shape=(
            jax.ShapeDtypeStruct((2 * groups, 2 * BINS), jnp.float32),
            jax.ShapeDtypeStruct((groups, 1), jnp.float32),
        ),
        name="lag_spectrum",
    )(jnp.swapaxes(correlation, 0, 1).reshape(2 * groups, length), forward)


def residual_kernel(half, own_ref, other_ref, spectrum_ref, weight_ref, forward_ref, inverse_ref, snr_ref, residual_ref, full_ref):
    section = lax.axis_index("sect")
    groups, share = residual_ref.shape
    samples = own_ref.shape[1]
    length = 2 * half + 1
    tiles = samples // LANES
    for tile in range(tiles):
        lanes = slice(tile * LANES, (tile + 1) * LANES)
        full_ref[tile] = own_ref[:, lanes] + other_ref[:, lanes]
    first = pl.multiple_of(section * share, share)
    mine = pl.ds(first, share)
    own_tiles = [section * (share // LANES) + step for step in range(share // LANES)]
    even = pl.ds(0, groups, stride=2)
    odd = pl.ds(1, groups, stride=2)

    def joined(rows, which):
        return jnp.concatenate([full_ref[tile, rows, :] for tile in which], axis=1)

    snr_ref[...] = joined(slice(None), own_tiles).astype(jnp.bfloat16)
    real_all = joined(even, range(tiles))
    imag_all = joined(odd, range(tiles))
    real_mid = joined(even, own_tiles)
    imag_mid = joined(odd, own_tiles)
    power = real_all * real_all + imag_all * imag_all
    high = power.astype(jnp.bfloat16)
    low = (power - high.astype(jnp.float32)).astype(jnp.bfloat16)
    source = lax.broadcasted_iota(jnp.int32, (samples, share), 0)
    target = lax.broadcasted_iota(jnp.int32, (samples, share), 1) + first
    band = (jnp.abs(source - target) <= half).astype(jnp.float32).astype(jnp.bfloat16)
    energy = jnp.dot(high, band, preferred_element_type=jnp.float32)
    energy += jnp.dot(low, band, preferred_element_type=jnp.float32)
    table = forward_ref[...]
    real_hat = jnp.dot(real_all.astype(jnp.bfloat16), table, preferred_element_type=jnp.float32)
    imag_hat = jnp.dot(imag_all.astype(jnp.bfloat16), table, preferred_element_type=jnp.float32)
    a_real, a_imag = real_hat[:, :BINS], real_hat[:, BINS:]
    b_real, b_imag = imag_hat[:, :BINS], imag_hat[:, BINS:]
    p_real, p_imag = spectrum_ref[0:groups, 0:BINS], spectrum_ref[0:groups, BINS:]
    q_real, q_imag = spectrum_ref[groups:, 0:BINS], spectrum_ref[groups:, BINS:]
    scale = jnp.float32(2.0 / PERIOD)
    back = inverse_ref[:, mine]

    def turned(low_part, high_part):
        parts = jnp.concatenate([low_part * scale, high_part * scale], axis=1).astype(jnp.bfloat16)
        return jnp.dot(parts, back, preferred_element_type=jnp.float32)

    real_sum = turned(
        a_real * p_real + a_imag * p_imag + b_real * q_real + b_imag * q_imag,
        a_imag * p_real - a_real * p_imag + b_imag * q_real - b_real * q_imag,
    )
    imag_sum = turned(
        b_real * p_real + b_imag * p_imag - a_real * q_real - a_imag * q_imag,
        b_imag * p_real - b_real * p_imag - a_imag * q_real + a_real * q_imag,
    )
    cross = real_mid * real_sum + imag_mid * imag_sum
    magnitude = real_mid * real_mid + imag_mid * imag_mid
    residual_ref[...] = (energy - 2.0 * cross + magnitude * weight_ref[...]) * jnp.float32(1.0 / (2.0 * length))


def residual_of(own, other, spectrum, weight, forward, inverse, half, share):
    columns = own.shape[0]
    return pl.pallas_call(
        functools.partial(residual_kernel, half),
        out_shape=(
            jax.ShapeDtypeStruct((columns, share), jnp.bfloat16),
            jax.ShapeDtypeStruct((columns // 2, share), jnp.float32),
        ),
        scratch_shapes=[pltpu.VMEM((own.shape[1] // LANES, columns, LANES), jnp.float32)],
        name="residual",
    )(own, other, spectrum, weight, forward, inverse)


def local(strain, filters, synthesis, correlation):
    sections = lax.axis_size("sect")
    chips = lax.axis_size("tmpl")
    taps = filters.shape[2]
    samples = strain.shape[1] - taps + 1
    share = samples // sections
    half = (correlation.shape[2] - 1) // 2
    forward = jnp.asarray(forward_matrix(samples), jnp.bfloat16)
    inverse = jnp.asarray(inverse_matrix(samples, half), jnp.bfloat16)
    basis = held_basis(strain, filters[0], samples)
    spectrum, weight = lag_spectrum(correlation, forward)
    block = jnp.broadcast_to(basis[None], (chips,) + basis.shape)
    piece = lax.all_to_all(block, "tmpl", 0, 0).reshape(-1, samples)
    own = jnp.dot(synthesis[0], piece, preferred_element_type=jnp.float32)
    other = lax.ppermute(own, "sect", [(0, 1), (1, 0)])
    return residual_of(own, other, spectrum, weight, forward, inverse, half, share)


def solution(mesh):
    placed = (
        P("sect", None),
        P("sect", "tmpl", None),
        P("sect", "tmpl", None),
        P("tmpl", None, None),
    )
    return jax.shard_map(
        local,
        mesh=mesh,
        in_specs=placed,
        out_specs=(P("tmpl", "sect"), P("tmpl", "sect")),
        check_vma=False,
    )
```

```python
import functools

import jax
import jax.numpy as jnp
import numpy as np
from jax import lax
from jax.experimental import pallas as pl
from jax.experimental.pallas import tpu as pltpu
from jax.sharding import PartitionSpec as P

KMAX = 4
PERIOD = 767
BINS = 384
LANES = 128
GRANT = 24 << 20


def forward_matrix(rows):
    angle = 2.0 * np.pi * np.outer(np.arange(rows), np.arange(BINS)) / PERIOD
    return np.concatenate([np.cos(angle), -np.sin(angle)], axis=1)


def inverse_matrix(samples, half):
    angle = 2.0 * np.pi * np.outer(np.arange(BINS), np.arange(samples) - half) / PERIOD
    share = np.where(np.arange(BINS) == 0, 0.5, 1.0)[:, None]
    return np.concatenate([share * np.cos(angle), -share * np.sin(angle)], axis=0)


def conv_kernel(strain_ref, filters_ref, basis_ref, line_ref):
    section = lax.axis_index("sect")
    taps = filters_ref.shape[1]
    samples = basis_ref.shape[2]
    width = line_ref.shape[1]
    rows = 256
    line_ref[...] = jnp.zeros_like(line_ref)
    line_ref[0:1, 0 : strain_ref.shape[1]] = strain_ref[...].astype(jnp.float32)
    spread = jnp.broadcast_to(line_ref[0:1, :], (rows, width))
    shifted = pltpu.roll(spread, width - (rows - 1), 1, stride=1, stride_axis=0).astype(jnp.bfloat16)
    row = lax.broadcasted_iota(jnp.int32, (rows, rows), 0)
    col = lax.broadcasted_iota(jnp.int32, (rows, rows), 1)
    flip = (row + col == rows - 1).astype(jnp.float32).astype(jnp.bfloat16)
    total = jnp.zeros((filters_ref.shape[0], samples), jnp.float32)
    for start in range(0, taps, rows):
        part = jnp.dot(filters_ref[:, start : start + rows], flip, preferred_element_type=jnp.float32)
        total += jnp.dot(
            part.astype(jnp.bfloat16), shifted[:, start : start + samples], preferred_element_type=jnp.float32
        )
    basis = total.astype(jnp.bfloat16)
    source = lax.broadcasted_iota(jnp.int32, (samples, samples), 0)
    target = lax.broadcasted_iota(jnp.int32, (samples, samples), 1)
    hold_log = lax.axis_size("sect") - 1 - section
    pick = (source == (target >> hold_log)).astype(jnp.float32).astype(jnp.bfloat16)
    held = jnp.dot(basis, pick, preferred_element_type=jnp.float32).astype(jnp.bfloat16)
    for chip in range(basis_ref.shape[0]):
        basis_ref[chip] = held


def held_basis(strain, filters, samples, chips):
    width = strain.shape[1] + 1
    return pl.pallas_call(
        conv_kernel,
        out_shape=jax.ShapeDtypeStruct((chips, filters.shape[0], samples), jnp.bfloat16),
        scratch_shapes=[pltpu.VMEM((8, width), jnp.float32)],
        compiler_params=pltpu.CompilerParams(vmem_limit_bytes=GRANT),
        name="held_basis",
    )(strain, filters)


def split(values):
    high = values.astype(jnp.bfloat16)
    return high, (values - high.astype(jnp.float32)).astype(jnp.bfloat16)


def rows_dot(left, right):
    return lax.dot_general(left, right, (((0,), (0,)), ((), ())), preferred_element_type=jnp.float32)


def lags_kernel(series_ref, forward_ref, spectrum_ref, weight_ref):
    length, pieces, lanes = series_ref.shape
    groups = weight_ref.shape[0]
    flat = series_ref.reshape(length * pieces, lanes)

    def part(which):
        halves = [flat[pl.ds(2 * tile + which, length, stride=pieces), :] for tile in range(pieces // 2)]
        return jnp.concatenate(halves, axis=1)

    real_part, imag_part = part(0), part(1)
    high, low = split(real_part * real_part + imag_part * imag_part)
    ones = jnp.ones((length, lanes), jnp.bfloat16)
    weight_ref[...] = rows_dot(high, ones) + rows_dot(low, ones)
    table = forward_ref[0:length, :]
    spectrum_ref[0:groups, :] = rows_dot(real_part.astype(jnp.bfloat16), table)
    spectrum_ref[groups:, :] = rows_dot(imag_part.astype(jnp.bfloat16), table)


def lag_spectrum(correlation, forward):
    groups, _, length = correlation.shape
    tiles = groups // LANES
    series = correlation.transpose(2, 1, 0).reshape(length, 2, tiles, LANES)
    series = series.transpose(0, 2, 1, 3).reshape(length, 2 * tiles, LANES)
    return pl.pallas_call(
        lags_kernel,
        out_shape=(
            jax.ShapeDtypeStruct((2 * groups, 2 * BINS), jnp.float32),
            jax.ShapeDtypeStruct((groups, LANES), jnp.float32),
        ),
        compiler_params=pltpu.CompilerParams(vmem_limit_bytes=GRANT),
        name="lag_spectrum",
    )(series, forward)


def residual_kernel(half, own_ref, other_ref, spectrum_ref, weight_ref, forward_ref, inverse_ref, snr_ref, residual_ref, full_ref):
    section = lax.axis_index("sect")
    groups, share = residual_ref.shape
    samples = own_ref.shape[1]
    length = 2 * half + 1
    tiles = samples // LANES
    for tile in range(tiles):
        lanes = slice(tile * LANES, (tile + 1) * LANES)
        full_ref[tile] = own_ref[:, lanes] + other_ref[:, lanes]
    first = pl.multiple_of(section * share, share)
    mine = pl.ds(first, share)
    own_tiles = [section * (share // LANES) + step for step in range(share // LANES)]
    even = pl.ds(0, groups, stride=2)
    odd = pl.ds(1, groups, stride=2)

    def joined(rows, which):
        return jnp.concatenate([full_ref[tile, rows, :] for tile in which], axis=1)

    snr_ref[...] = joined(slice(None), own_tiles).astype(jnp.bfloat16)
    real_all = joined(even, range(tiles))
    imag_all = joined(odd, range(tiles))
    real_mid = joined(even, own_tiles)
    imag_mid = joined(odd, own_tiles)
    power = real_all * real_all + imag_all * imag_all
    high, low = split(power)
    source = lax.broadcasted_iota(jnp.int32, (samples, share), 0)
    target = lax.broadcasted_iota(jnp.int32, (samples, share), 1) + first
    band = (jnp.abs(source - target) <= half).astype(jnp.float32).astype(jnp.bfloat16)
    energy = jnp.dot(high, band, preferred_element_type=jnp.float32)
    energy += jnp.dot(low, band, preferred_element_type=jnp.float32)
    table = forward_ref[...]
    real_hat = jnp.dot(real_all.astype(jnp.bfloat16), table, preferred_element_type=jnp.float32)
    imag_hat = jnp.dot(imag_all.astype(jnp.bfloat16), table, preferred_element_type=jnp.float32)
    a_real, a_imag = real_hat[:, :BINS], real_hat[:, BINS:]
    b_real, b_imag = imag_hat[:, :BINS], imag_hat[:, BINS:]
    p_real, p_imag = spectrum_ref[0:groups, 0:BINS], spectrum_ref[0:groups, BINS:]
    q_real, q_imag = spectrum_ref[groups:, 0:BINS], spectrum_ref[groups:, BINS:]
    scale = jnp.float32(2.0 / PERIOD)
    back = inverse_ref[:, mine]

    def turned(low_part, high_part):
        parts = jnp.concatenate([low_part * scale, high_part * scale], axis=1).astype(jnp.bfloat16)
        return jnp.dot(parts, back, preferred_element_type=jnp.float32)

    real_sum = turned(
        a_real * p_real + a_imag * p_imag + b_real * q_real + b_imag * q_imag,
        a_imag * p_real - a_real * p_imag + b_imag * q_real - b_real * q_imag,
    )
    imag_sum = turned(
        b_real * p_real + b_imag * p_imag - a_real * q_real - a_imag * q_imag,
        b_imag * p_real - b_real * p_imag - a_imag * q_real + a_real * q_imag,
    )
    cross = real_mid * real_sum + imag_mid * imag_sum
    magnitude = real_mid * real_mid + imag_mid * imag_mid
    weight = jnp.concatenate([weight_ref[...]] * (share // LANES), axis=1)
    residual_ref[...] = (energy - 2.0 * cross + magnitude * weight) * jnp.float32(1.0 / (2.0 * length))


def residual_of(own, other, spectrum, weight, forward, inverse, half, share):
    columns = own.shape[0]
    return pl.pallas_call(
        functools.partial(residual_kernel, half),
        out_shape=(
            jax.ShapeDtypeStruct((columns, share), jnp.bfloat16),
            jax.ShapeDtypeStruct((columns // 2, share), jnp.float32),
        ),
        scratch_shapes=[pltpu.VMEM((own.shape[1] // LANES, columns, LANES), jnp.float32)],
        compiler_params=pltpu.CompilerParams(vmem_limit_bytes=GRANT),
        name="residual",
    )(own, other, spectrum, weight, forward, inverse)


def local(strain, filters, synthesis, correlation):
    sections = lax.axis_size("sect")
    chips = lax.axis_size("tmpl")
    taps = filters.shape[2]
    samples = strain.shape[1] - taps + 1
    share = samples // sections
    half = (correlation.shape[2] - 1) // 2
    forward = jnp.asarray(forward_matrix(samples), jnp.bfloat16)
    inverse = jnp.asarray(inverse_matrix(samples, half), jnp.bfloat16)
    block = held_basis(strain, filters[0], samples, chips)
    spectrum, weight = lag_spectrum(correlation, forward)
    piece = lax.all_to_all(block, "tmpl", 0, 0).reshape(-1, samples)
    own = jnp.dot(synthesis[0], piece, preferred_element_type=jnp.float32)
    other = lax.ppermute(own, "sect", [(0, 1), (1, 0)])
    return residual_of(own, other, spectrum, weight, forward, inverse, half, share)


def solution(mesh):
    placed = (
        P("sect", None),
        P("sect", "tmpl", None),
        P("sect", "tmpl", None),
        P("tmpl", None, None),
    )
    return jax.shard_map(
        local,
        mesh=mesh,
        in_specs=placed,
        out_specs=(P("tmpl", "sect"), P("tmpl", "sect")),
        check_vma=False,
    )
```

```python
import functools

import jax
import jax.numpy as jnp
import numpy as np
from jax import lax
from jax.experimental import pallas as pl
from jax.experimental.pallas import tpu as pltpu
from jax.sharding import PartitionSpec as P


PERIOD = 767
BINS = 384
LANES = 128
GRANT = 24 << 20


def forward_matrix(rows):
    angle = 2.0 * np.pi * np.outer(np.arange(rows), np.arange(BINS)) / PERIOD
    return np.concatenate([np.cos(angle), -np.sin(angle)], axis=1)


def inverse_matrix(samples, half):
    angle = 2.0 * np.pi * np.outer(np.arange(BINS), np.arange(samples) - half) / PERIOD
    share = np.where(np.arange(BINS) == 0, 0.5, 1.0)[:, None]
    return np.concatenate([share * np.cos(angle), -share * np.sin(angle)], axis=0)


def convolved(line, bank, count):
    rows = 256
    taps = bank.shape[1]
    width = line.shape[1]
    row = lax.broadcasted_iota(jnp.int32, (rows, rows), 0)
    col = lax.broadcasted_iota(jnp.int32, (rows, rows), 1)
    flip = (row + col == rows - 1).astype(jnp.float32).astype(jnp.bfloat16)
    spread = jnp.broadcast_to(line, (rows, width))
    shifted = pltpu.roll(spread, width - (rows - 1), 1, stride=1, stride_axis=0).astype(jnp.bfloat16)
    total = jnp.zeros((bank.shape[0], count), jnp.float32)
    for start in range(0, taps, rows):
        part = jnp.dot(bank[:, start : start + rows], flip, preferred_element_type=jnp.float32)
        total += jnp.dot(
            part.astype(jnp.bfloat16), shifted[:, start : start + count], preferred_element_type=jnp.float32
        )
    return total.astype(jnp.bfloat16)


def first_kernel(line_hbm, bank_hbm, basis_ref, raw_ref, bank_ref, line_ref, sems):
    section = lax.axis_index("sect")
    taps = bank_ref.shape[1]
    wide = basis_ref.shape[1]
    line_copy = pltpu.make_async_copy(line_hbm, raw_ref, sems.at[0])
    bank_copy = pltpu.make_async_copy(bank_hbm, bank_ref, sems.at[1])
    line_copy.start()
    bank_copy.start()
    line_copy.wait()
    line_ref[...] = jnp.zeros_like(line_ref)
    line_ref[0:1, 0 : raw_ref.shape[1]] = raw_ref[...].astype(jnp.float32)
    begin = pl.multiple_of(section * LANES, LANES)
    line = line_ref[0:1, pl.ds(begin, taps + wide)]
    bank_copy.wait()
    basis_ref[...] = convolved(line, bank_ref[...], wide)


def first_columns(line, bank, wide):
    width = line.shape[1] + 1
    return pl.pallas_call(
        first_kernel,
        in_specs=[pl.BlockSpec(memory_space=pltpu.HBM)] * 2,
        out_shape=jax.ShapeDtypeStruct((bank.shape[0], wide), jnp.bfloat16),
        scratch_shapes=[
            pltpu.VMEM(line.shape, line.dtype),
            pltpu.VMEM(bank.shape, bank.dtype),
            pltpu.VMEM((8, width), jnp.float32),
            pltpu.SemaphoreType.DMA((2,)),
        ],
        compiler_params=pltpu.CompilerParams(vmem_limit_bytes=GRANT),
        cost_estimate=pl.CostEstimate(flops=1 << 30, bytes_accessed=1 << 22, transcendentals=0),
        name="first_columns",
    )(line, bank)


def last_kernel(own_line_ref, other_line_ref, own_ref, other_ref, first_ref, basis_ref, line_ref):
    section = lax.axis_index("sect")
    taps = own_ref.shape[1]
    share = basis_ref.shape[2]
    length = own_line_ref.shape[1]
    line_ref[...] = jnp.zeros_like(line_ref)
    line_ref[0:1, 0:length] = own_line_ref[...].astype(jnp.float32)
    line_ref[8:9, 0:length] = other_line_ref[...].astype(jnp.float32)
    own = line_ref[0:1, share : share + taps + LANES]
    line = jnp.where(section == 0, line_ref[8:9, 0 : taps + LANES], own)
    bank = jnp.where(section == 0, other_ref[...].astype(jnp.float32), own_ref[...].astype(jnp.float32))
    last = convolved(line, bank.astype(jnp.bfloat16), LANES)
    basis = jnp.concatenate([first_ref[...], last], axis=1)
    for chip in range(basis_ref.shape[0]):
        basis_ref[chip] = basis


def basis_share(own_line, other_line, own, other, first, chips):
    width = own_line.shape[1] + 1
    share = first.shape[1] + LANES
    return pl.pallas_call(
        last_kernel,
        out_shape=jax.ShapeDtypeStruct((chips, own.shape[0], share), jnp.bfloat16),
        scratch_shapes=[pltpu.VMEM((16, width), jnp.float32)],
        compiler_params=pltpu.CompilerParams(vmem_limit_bytes=GRANT),
        name="basis_share",
    )(own_line, other_line, own, other, first)


def split(values):
    high = values.astype(jnp.bfloat16)
    return high, (values - high.astype(jnp.float32)).astype(jnp.bfloat16)


def rows_dot(left, right):
    return lax.dot_general(left, right, (((0,), (0,)), ((), ())), preferred_element_type=jnp.float32)


def products(rows_ref, fast_own_ref, fast_other_ref, basis_ref, out_ref):
    section = lax.axis_index("sect")
    wide = basis_ref.shape[1] - LANES
    out_ref[:, 0:wide] = jnp.dot(rows_ref[...], basis_ref[:, 0:wide], preferred_element_type=jnp.float32)

    @pl.when(section == 0)
    def _():
        out_ref[:, wide:] = jnp.dot(fast_other_ref[...], basis_ref[:, wide:], preferred_element_type=jnp.float32)

    @pl.when(section == 1)
    def _():
        out_ref[:, wide:] = jnp.dot(fast_own_ref[...], basis_ref[:, wide:], preferred_element_type=jnp.float32)


def lags_kernel(series_ref, forward_ref, spectrum_ref, weight_ref):
    length, pieces, lanes = series_ref.shape
    groups = weight_ref.shape[0]
    flat = series_ref.reshape(length * pieces, lanes)

    def part(which):
        halves = [flat[pl.ds(2 * tile + which, length, stride=pieces), :] for tile in range(pieces // 2)]
        return jnp.concatenate(halves, axis=1)

    real_part, imag_part = part(0), part(1)
    high, low = split(real_part * real_part + imag_part * imag_part)
    ones = jnp.ones((length, lanes), jnp.bfloat16)
    weight_ref[...] = rows_dot(high, ones) + rows_dot(low, ones)
    table = forward_ref[0:length, :]
    spectrum_ref[0:groups, :] = rows_dot(real_part.astype(jnp.bfloat16), table)
    spectrum_ref[groups:, :] = rows_dot(imag_part.astype(jnp.bfloat16), table)


def lag_spectrum(correlation, forward):
    groups, _, length = correlation.shape
    tiles = groups // LANES
    series = correlation.transpose(2, 1, 0).reshape(length, 2, tiles, LANES)
    series = series.transpose(0, 2, 1, 3).reshape(length, 2 * tiles, LANES)
    return pl.pallas_call(
        lags_kernel,
        out_shape=(
            jax.ShapeDtypeStruct((2 * groups, 2 * BINS), jnp.float32),
            jax.ShapeDtypeStruct((groups, LANES), jnp.float32),
        ),
        compiler_params=pltpu.CompilerParams(vmem_limit_bytes=GRANT),
        cost_estimate=pl.CostEstimate(flops=1 << 30, bytes_accessed=1 << 22, transcendentals=0),
        name="lag_spectrum",
    )(series, forward)


def share_products(own, other, basis):
    columns = own.shape[0]
    share = basis.shape[1]
    return pl.pallas_call(
        lambda own_ref, other_ref, basis_ref, out_ref: products(own_ref, own_ref, other_ref, basis_ref, out_ref),
        out_shape=jax.ShapeDtypeStruct((columns, share), jnp.float32),
        compiler_params=pltpu.CompilerParams(vmem_limit_bytes=GRANT),
        cost_estimate=pl.CostEstimate(flops=1 << 30, bytes_accessed=1 << 22, transcendentals=0),
        name="share_products",
    )(own, other, basis)


def residual_kernel(
    half,
    own_ref,
    other_ref,
    basis_ref,
    part_ref,
    spectrum_ref,
    weight_ref,
    forward_ref,
    inverse_ref,
    snr_ref,
    residual_ref,
    full_ref,
    rest_ref,
    slow_ref,
):
    section = lax.axis_index("sect")
    groups, share = residual_ref.shape
    samples = forward_ref.shape[0]
    length = 2 * half + 1
    tiles = samples // LANES
    wide = basis_ref.shape[1] - LANES
    products(other_ref, own_ref, other_ref, basis_ref, rest_ref)

    def placed(slow, middle, left, right):
        slow_ref[...] = slow[:, 0:wide]
        full_ref[0] = left[:, wide:]
        for tile in range(1, tiles - 1):
            full_ref[tile] = middle[:, (tile - 1) * LANES : tile * LANES]
        full_ref[tiles - 1] = right[:, wide:]

    @pl.when(section == 0)
    def _():
        placed(part_ref, rest_ref, part_ref, rest_ref)

    @pl.when(section == 1)
    def _():
        placed(rest_ref, part_ref, rest_ref, part_ref)

    source = lax.broadcasted_iota(jnp.int32, (wide, samples), 0)
    target = lax.broadcasted_iota(jnp.int32, (wide, samples), 1)
    hold = (source == target // 2).astype(jnp.float32).astype(jnp.bfloat16)
    high, low = split(slow_ref[...])
    held = jnp.dot(high, hold, preferred_element_type=jnp.float32)
    held += jnp.dot(low, hold, preferred_element_type=jnp.float32)
    for tile in range(tiles):
        full_ref[tile] += held[:, tile * LANES : (tile + 1) * LANES]
    first = pl.multiple_of(section * share, share)
    mine = pl.ds(first, share)
    own_tiles = [section * (share // LANES) + step for step in range(share // LANES)]
    even = pl.ds(0, groups, stride=2)
    odd = pl.ds(1, groups, stride=2)

    def joined(rows, which):
        return jnp.concatenate([full_ref[tile, rows, :] for tile in which], axis=1)

    snr_ref[...] = joined(slice(None), own_tiles).astype(jnp.bfloat16)
    real_all = joined(even, range(tiles))
    imag_all = joined(odd, range(tiles))
    real_mid = joined(even, own_tiles)
    imag_mid = joined(odd, own_tiles)
    power = real_all * real_all + imag_all * imag_all
    high, low = split(power)
    source = lax.broadcasted_iota(jnp.int32, (samples, share), 0)
    target = lax.broadcasted_iota(jnp.int32, (samples, share), 1) + first
    band = (jnp.abs(source - target) <= half).astype(jnp.float32).astype(jnp.bfloat16)
    energy = jnp.dot(high, band, preferred_element_type=jnp.float32)
    energy += jnp.dot(low, band, preferred_element_type=jnp.float32)
    table = forward_ref[...]
    real_hat = jnp.dot(real_all.astype(jnp.bfloat16), table, preferred_element_type=jnp.float32)
    imag_hat = jnp.dot(imag_all.astype(jnp.bfloat16), table, preferred_element_type=jnp.float32)
    a_real, a_imag = real_hat[:, :BINS], real_hat[:, BINS:]
    b_real, b_imag = imag_hat[:, :BINS], imag_hat[:, BINS:]
    p_real, p_imag = spectrum_ref[0:groups, 0:BINS], spectrum_ref[0:groups, BINS:]
    q_real, q_imag = spectrum_ref[groups:, 0:BINS], spectrum_ref[groups:, BINS:]
    scale = jnp.float32(2.0 / PERIOD)
    back = inverse_ref[:, mine]

    def turned(low_part, high_part):
        parts = jnp.concatenate([low_part * scale, high_part * scale], axis=1).astype(jnp.bfloat16)
        return jnp.dot(parts, back, preferred_element_type=jnp.float32)

    real_sum = turned(
        a_real * p_real + a_imag * p_imag + b_real * q_real + b_imag * q_imag,
        a_imag * p_real - a_real * p_imag + b_imag * q_real - b_real * q_imag,
    )
    imag_sum = turned(
        b_real * p_real + b_imag * p_imag - a_real * q_real - a_imag * q_imag,
        b_imag * p_real - b_real * p_imag - a_imag * q_real + a_real * q_imag,
    )
    cross = real_mid * real_sum + imag_mid * imag_sum
    magnitude = real_mid * real_mid + imag_mid * imag_mid
    weight = jnp.concatenate([weight_ref[...]] * (share // LANES), axis=1)
    residual_ref[...] = (energy - 2.0 * cross + magnitude * weight) * jnp.float32(1.0 / (2.0 * length))


def residual_of(own, other, basis, part, spectrum, weight, forward, inverse, half, share):
    columns = own.shape[0]
    wide = basis.shape[1] - LANES
    return pl.pallas_call(
        functools.partial(residual_kernel, half),
        out_shape=(
            jax.ShapeDtypeStruct((columns, share), jnp.bfloat16),
            jax.ShapeDtypeStruct((columns // 2, share), jnp.float32),
        ),
        scratch_shapes=[
            pltpu.VMEM((forward.shape[0] // LANES, columns, LANES), jnp.float32),
            pltpu.VMEM(part.shape, jnp.float32),
            pltpu.VMEM((columns, wide), jnp.float32),
        ],
        compiler_params=pltpu.CompilerParams(vmem_limit_bytes=GRANT),
        name="residual",
    )(own, other, basis, part, spectrum, weight, forward, inverse)


def local(strain, filters, synthesis, correlation):
    sections = lax.axis_size("sect")
    chips = lax.axis_size("tmpl")
    taps = filters.shape[2]
    samples = strain.shape[1] - taps + 1
    half = (correlation.shape[2] - 1) // 2
    share = (samples + samples // 2) // sections
    swap = [(0, 1), (1, 0)]
    forward = jnp.asarray(forward_matrix(samples), jnp.bfloat16)
    inverse = jnp.asarray(inverse_matrix(samples, half), jnp.bfloat16)
    own_bank = filters[0]
    own_rows = synthesis[0]
    other_line = lax.ppermute(strain, "sect", swap)
    other_bank = lax.ppermute(own_bank, "sect", swap)
    other_rows = lax.ppermute(own_rows, "sect", swap)
    first = first_columns(strain, own_bank, share - LANES)
    block = basis_share(strain, other_line, own_bank, other_bank, first, chips)
    mine = lax.all_to_all(block, "tmpl", 0, 0).reshape(-1, share)
    theirs = lax.ppermute(mine, "sect", swap)
    spectrum, weight = lag_spectrum(correlation, forward)
    part = share_products(own_rows, other_rows, mine)
    return residual_of(
        own_rows, other_rows, theirs, part, spectrum, weight, forward, inverse, half, samples // sections
    )


def solution(mesh):
    placed = (
        P("sect", None),
        P("sect", "tmpl", None),
        P("sect", "tmpl", None),
        P("tmpl", None, None),
    )
    return jax.shard_map(
        local,
        mesh=mesh,
        in_specs=placed,
        out_specs=(P("tmpl", "sect"), P("tmpl", "sect")),
        check_vma=False,
    )
```

```python
import functools

import jax
import jax.numpy as jnp
import numpy as np
from jax import lax
from jax.experimental import pallas as pl
from jax.experimental.pallas import tpu as pltpu
from jax.sharding import PartitionSpec as P


PERIOD = 767
BINS = 384
LANES = 128
GRANT = 24 << 20


def forward_matrix(rows):
    angle = 2.0 * np.pi * np.outer(np.arange(rows), np.arange(BINS)) / PERIOD
    return np.concatenate([np.cos(angle), -np.sin(angle)], axis=1)


def inverse_matrix(samples, half):
    angle = 2.0 * np.pi * np.outer(np.arange(BINS), np.arange(samples) - half) / PERIOD
    share = np.where(np.arange(BINS) == 0, 0.5, 1.0)[:, None]
    return np.concatenate([share * np.cos(angle), -share * np.sin(angle)], axis=0)


def convolved(line, bank, count):
    rows = 256
    taps = bank.shape[1]
    width = line.shape[1]
    row = lax.broadcasted_iota(jnp.int32, (rows, rows), 0)
    col = lax.broadcasted_iota(jnp.int32, (rows, rows), 1)
    flip = (row + col == rows - 1).astype(jnp.float32).astype(jnp.bfloat16)
    spread = jnp.broadcast_to(line, (rows, width))
    shifted = pltpu.roll(spread, width - (rows - 1), 1, stride=1, stride_axis=0).astype(jnp.bfloat16)
    total = jnp.zeros((bank.shape[0], count), jnp.float32)
    for start in range(0, taps, rows):
        part = jnp.dot(bank[:, start : start + rows], flip, preferred_element_type=jnp.float32)
        total += jnp.dot(
            part.astype(jnp.bfloat16), shifted[:, start : start + count], preferred_element_type=jnp.float32
        )
    return total.astype(jnp.bfloat16)


def first_kernel(line_hbm, bank_hbm, basis_ref, raw_ref, bank_ref, line_ref, sems):
    section = lax.axis_index("sect")
    taps = bank_ref.shape[1]
    wide = basis_ref.shape[1]
    line_copy = pltpu.make_async_copy(line_hbm, raw_ref, sems.at[0])
    bank_copy = pltpu.make_async_copy(bank_hbm, bank_ref, sems.at[1])
    line_copy.start()
    bank_copy.start()
    line_copy.wait()
    line_ref[...] = jnp.zeros_like(line_ref)
    line_ref[0:1, 0 : raw_ref.shape[1]] = raw_ref[...].astype(jnp.float32)
    begin = pl.multiple_of(section * LANES, LANES)
    line = line_ref[0:1, pl.ds(begin, taps + wide)]
    bank_copy.wait()
    basis_ref[...] = convolved(line, bank_ref[...], wide)


def first_columns(line, bank, wide):
    width = line.shape[1] + 1
    return pl.pallas_call(
        first_kernel,
        in_specs=[pl.BlockSpec(memory_space=pltpu.HBM)] * 2,
        out_shape=jax.ShapeDtypeStruct((bank.shape[0], wide), jnp.bfloat16),
        scratch_shapes=[
            pltpu.VMEM(line.shape, line.dtype),
            pltpu.VMEM(bank.shape, bank.dtype),
            pltpu.VMEM((8, width), jnp.float32),
            pltpu.SemaphoreType.DMA((2,)),
        ],
        compiler_params=pltpu.CompilerParams(vmem_limit_bytes=GRANT),
        cost_estimate=pl.CostEstimate(flops=1 << 30, bytes_accessed=1 << 22, transcendentals=0),
        name="first_columns",
    )(pltpu.with_memory_space_constraint(line, pltpu.HBM), pltpu.with_memory_space_constraint(bank, pltpu.HBM))


def last_kernel(own_line_ref, other_line_ref, own_ref, other_ref, first_ref, basis_ref, line_ref):
    section = lax.axis_index("sect")
    taps = own_ref.shape[1]
    share = basis_ref.shape[2]
    length = own_line_ref.shape[1]
    line_ref[...] = jnp.zeros_like(line_ref)
    line_ref[0:1, 0:length] = own_line_ref[...].astype(jnp.float32)
    line_ref[8:9, 0:length] = other_line_ref[...].astype(jnp.float32)
    own = line_ref[0:1, share : share + taps + LANES]
    line = jnp.where(section == 0, line_ref[8:9, 0 : taps + LANES], own)
    bank = jnp.where(section == 0, other_ref[...].astype(jnp.float32), own_ref[...].astype(jnp.float32))
    last = convolved(line, bank.astype(jnp.bfloat16), LANES)
    basis = jnp.concatenate([first_ref[...], last], axis=1)
    for chip in range(basis_ref.shape[0]):
        basis_ref[chip] = basis


def basis_share(own_line, other_line, own, other, first, chips):
    width = own_line.shape[1] + 1
    share = first.shape[1] + LANES
    return pl.pallas_call(
        last_kernel,
        out_shape=jax.ShapeDtypeStruct((chips, own.shape[0], share), jnp.bfloat16),
        scratch_shapes=[pltpu.VMEM((16, width), jnp.float32)],
        compiler_params=pltpu.CompilerParams(vmem_limit_bytes=GRANT),
        name="basis_share",
    )(own_line, other_line, own, other, first)


def split(values):
    high = values.astype(jnp.bfloat16)
    return high, (values - high.astype(jnp.float32)).astype(jnp.bfloat16)


def rows_dot(left, right):
    return lax.dot_general(left, right, (((0,), (0,)), ((), ())), preferred_element_type=jnp.float32)


def products(rows_ref, fast_own_ref, fast_other_ref, basis_ref, out_ref):
    section = lax.axis_index("sect")
    wide = basis_ref.shape[1] - LANES
    out_ref[:, 0:wide] = jnp.dot(rows_ref[...], basis_ref[:, 0:wide], preferred_element_type=jnp.float32)

    @pl.when(section == 0)
    def _():
        out_ref[:, wide:] = jnp.dot(fast_other_ref[...], basis_ref[:, wide:], preferred_element_type=jnp.float32)

    @pl.when(section == 1)
    def _():
        out_ref[:, wide:] = jnp.dot(fast_own_ref[...], basis_ref[:, wide:], preferred_element_type=jnp.float32)


def lags_kernel(series_ref, forward_ref, spectrum_ref, weight_ref):
    length, pieces, lanes = series_ref.shape
    groups = weight_ref.shape[0]
    flat = series_ref.reshape(length * pieces, lanes)

    def part(which):
        halves = [flat[pl.ds(2 * tile + which, length, stride=pieces), :] for tile in range(pieces // 2)]
        return jnp.concatenate(halves, axis=1)

    real_part, imag_part = part(0), part(1)
    high, low = split(real_part * real_part + imag_part * imag_part)
    ones = jnp.ones((length, lanes), jnp.bfloat16)
    weight_ref[...] = rows_dot(high, ones) + rows_dot(low, ones)
    table = forward_ref[0:length, :]
    scale = jnp.float32(1.0 / PERIOD)
    real_hat = rows_dot(real_part.astype(jnp.bfloat16), table) * scale
    imag_hat = rows_dot(imag_part.astype(jnp.bfloat16), table) * scale
    spectrum_ref[0:groups, 0:BINS] = real_hat[:, :BINS] - imag_hat[:, BINS:]
    spectrum_ref[0:groups, BINS:] = real_hat[:, BINS:] + imag_hat[:, :BINS]
    spectrum_ref[groups:, 0:BINS] = real_hat[:, :BINS] + imag_hat[:, BINS:]
    spectrum_ref[groups:, BINS:] = real_hat[:, BINS:] - imag_hat[:, :BINS]


def lag_spectrum(correlation, forward):
    groups, _, length = correlation.shape
    tiles = groups // LANES
    series = correlation.transpose(2, 1, 0).reshape(length, 2, tiles, LANES)
    series = series.transpose(0, 2, 1, 3).reshape(length, 2 * tiles, LANES)
    return pl.pallas_call(
        lags_kernel,
        out_shape=(
            jax.ShapeDtypeStruct((2 * groups, 2 * BINS), jnp.float32),
            jax.ShapeDtypeStruct((groups, LANES), jnp.float32),
        ),
        compiler_params=pltpu.CompilerParams(vmem_limit_bytes=GRANT),
        cost_estimate=pl.CostEstimate(flops=1 << 30, bytes_accessed=1 << 22, transcendentals=0),
        name="lag_spectrum",
    )(series, forward)


def share_products(own, other, basis):
    columns = own.shape[0]
    share = basis.shape[1]
    return pl.pallas_call(
        lambda own_ref, other_ref, basis_ref, out_ref: products(own_ref, own_ref, other_ref, basis_ref, out_ref),
        out_shape=jax.ShapeDtypeStruct((columns, share), jnp.float32),
        compiler_params=pltpu.CompilerParams(vmem_limit_bytes=GRANT),
        cost_estimate=pl.CostEstimate(flops=1 << 30, bytes_accessed=1 << 22, transcendentals=0),
        name="share_products",
    )(own, other, basis)


def residual_kernel(
    half,
    own_ref,
    other_ref,
    basis_ref,
    part_ref,
    spectrum_ref,
    weight_ref,
    forward_ref,
    inverse_ref,
    snr_ref,
    residual_ref,
    full_ref,
    rest_ref,
):
    section = lax.axis_index("sect")
    groups, share = residual_ref.shape
    samples = forward_ref.shape[0]
    length = 2 * half + 1
    tiles = samples // LANES
    wide = basis_ref.shape[1] - LANES
    products(other_ref, own_ref, other_ref, basis_ref, rest_ref)

    lane = lax.broadcasted_iota(jnp.int32, (2 * groups, LANES), 1)

    def placed(slow, middle, left, right):
        for tile in range(tiles):
            start = (tile // 2) * LANES
            held = jnp.take_along_axis(slow[:, start : start + LANES], lane // 2 + (tile % 2) * (LANES // 2), axis=1)
            if tile == 0:
                fast = left[:, wide:]
            elif tile == tiles - 1:
                fast = right[:, wide:]
            else:
                fast = middle[:, (tile - 1) * LANES : tile * LANES]
            full_ref[tile] = held + fast

    @pl.when(section == 0)
    def _():
        placed(part_ref, rest_ref, part_ref, rest_ref)

    @pl.when(section == 1)
    def _():
        placed(rest_ref, part_ref, rest_ref, part_ref)

    first = pl.multiple_of(section * share, share)
    mine = pl.ds(first, share)
    own_tiles = [section * (share // LANES) + step for step in range(share // LANES)]
    even = pl.ds(0, groups, stride=2)
    odd = pl.ds(1, groups, stride=2)

    def joined(rows, which):
        return jnp.concatenate([full_ref[tile, rows, :] for tile in which], axis=1)

    snr_ref[...] = joined(slice(None), own_tiles).astype(jnp.bfloat16)
    real_all = joined(even, range(tiles))
    imag_all = joined(odd, range(tiles))
    real_mid = joined(even, own_tiles)
    imag_mid = joined(odd, own_tiles)
    power = real_all * real_all + imag_all * imag_all
    high, low = split(power)
    source = lax.broadcasted_iota(jnp.int32, (samples, share), 0)
    target = lax.broadcasted_iota(jnp.int32, (samples, share), 1) + first
    band = (jnp.abs(source - target) <= half).astype(jnp.float32).astype(jnp.bfloat16)
    energy = jnp.dot(high, band, preferred_element_type=jnp.float32)
    energy += jnp.dot(low, band, preferred_element_type=jnp.float32)
    table = forward_ref[...]
    real_hat = jnp.dot(real_all.astype(jnp.bfloat16), table, preferred_element_type=jnp.float32)
    imag_hat = jnp.dot(imag_all.astype(jnp.bfloat16), table, preferred_element_type=jnp.float32)
    a_real, a_imag = real_hat[:, :BINS], real_hat[:, BINS:]
    b_real, b_imag = imag_hat[:, :BINS], imag_hat[:, BINS:]
    p_real, p_imag = spectrum_ref[0:groups, 0:BINS], spectrum_ref[0:groups, BINS:]
    q_real, q_imag = spectrum_ref[groups:, 0:BINS], spectrum_ref[groups:, BINS:]
    back = inverse_ref[:, mine]

    def turned(low_part, high_part):
        parts = jnp.concatenate([low_part, high_part], axis=1).astype(jnp.bfloat16)
        return jnp.dot(parts, back, preferred_element_type=jnp.float32)

    up_real, up_imag = a_real - b_imag, a_imag + b_real
    down_real, down_imag = a_real + b_imag, a_imag - b_real
    plus_real = up_real * p_real + up_imag * p_imag
    plus_imag = up_imag * p_real - up_real * p_imag
    minus_real = down_real * q_real + down_imag * q_imag
    minus_imag = down_imag * q_real - down_real * q_imag
    real_sum = turned(plus_real + minus_real, plus_imag + minus_imag)
    imag_sum = turned(plus_imag - minus_imag, minus_real - plus_real)
    cross = real_mid * real_sum + imag_mid * imag_sum
    magnitude = real_mid * real_mid + imag_mid * imag_mid
    weight = jnp.concatenate([weight_ref[...]] * (share // LANES), axis=1)
    residual_ref[...] = (energy - 2.0 * cross + magnitude * weight) * jnp.float32(1.0 / (2.0 * length))


def residual_of(own, other, basis, part, spectrum, weight, forward, inverse, half, share):
    columns = own.shape[0]
    return pl.pallas_call(
        functools.partial(residual_kernel, half),
        out_shape=(
            jax.ShapeDtypeStruct((columns, share), jnp.bfloat16),
            jax.ShapeDtypeStruct((columns // 2, share), jnp.float32),
        ),
        scratch_shapes=[
            pltpu.VMEM((forward.shape[0] // LANES, columns, LANES), jnp.float32),
            pltpu.VMEM(part.shape, jnp.float32),
        ],
        compiler_params=pltpu.CompilerParams(vmem_limit_bytes=GRANT),
        name="residual",
    )(own, other, basis, part, spectrum, weight, forward, inverse)


def local(strain, filters, synthesis, correlation):
    sections = lax.axis_size("sect")
    chips = lax.axis_size("tmpl")
    taps = filters.shape[2]
    samples = strain.shape[1] - taps + 1
    half = (correlation.shape[2] - 1) // 2
    share = (samples + samples // 2) // sections
    swap = [(0, 1), (1, 0)]
    forward = jnp.asarray(forward_matrix(samples), jnp.bfloat16)
    inverse = jnp.asarray(inverse_matrix(samples, half), jnp.bfloat16)
    own_bank = filters[0]
    own_rows = synthesis[0]
    other_line = lax.ppermute(strain, "sect", swap)
    other_bank = lax.ppermute(own_bank, "sect", swap)
    other_rows = lax.ppermute(own_rows, "sect", swap)
    first = first_columns(strain, own_bank, share - LANES)
    block = basis_share(strain, other_line, own_bank, other_bank, first, chips)
    mine = lax.all_to_all(block, "tmpl", 0, 0).reshape(-1, share)
    theirs = lax.ppermute(mine, "sect", swap)
    spectrum, weight = lag_spectrum(correlation, forward)
    part = share_products(own_rows, other_rows, mine)
    return residual_of(
        own_rows, other_rows, theirs, part, spectrum, weight, forward, inverse, half, samples // sections
    )


def solution(mesh):
    placed = (
        P("sect", None),
        P("sect", "tmpl", None),
        P("sect", "tmpl", None),
        P("tmpl", None, None),
    )
    return jax.shard_map(
        local,
        mesh=mesh,
        in_specs=placed,
        out_specs=(P("tmpl", "sect"), P("tmpl", "sect")),
        check_vma=False,
    )
```

```python
import functools

import jax
import jax.numpy as jnp
import numpy as np
from jax import lax
from jax.experimental import pallas as pl
from jax.experimental.pallas import tpu as pltpu
from jax.sharding import PartitionSpec as P


PERIOD = 767
BINS = 384
LANES = 128
GRANT = 24 << 20
SENT = jnp.float32


def forward_matrix(rows):
    angle = 2.0 * np.pi * np.outer(np.arange(rows), np.arange(BINS)) / PERIOD
    return np.concatenate([np.cos(angle), -np.sin(angle)], axis=1)


def inverse_matrix(samples, half):
    angle = 2.0 * np.pi * np.outer(np.arange(BINS), np.arange(samples) - half) / PERIOD
    share = np.where(np.arange(BINS) == 0, 0.5, 1.0)[:, None]
    return np.concatenate([share * np.cos(angle), -share * np.sin(angle)], axis=0)


def convolved(line, bank, count):
    rows = 256
    taps = bank.shape[1]
    width = line.shape[1]
    row = lax.broadcasted_iota(jnp.int32, (rows, rows), 0)
    col = lax.broadcasted_iota(jnp.int32, (rows, rows), 1)
    flip = (row + col == rows - 1).astype(jnp.float32).astype(jnp.bfloat16)
    spread = jnp.broadcast_to(line, (rows, width))
    shifted = pltpu.roll(spread, width - (rows - 1), 1, stride=1, stride_axis=0).astype(jnp.bfloat16)
    total = jnp.zeros((bank.shape[0], count), jnp.float32)
    for start in range(0, taps, rows):
        part = jnp.dot(bank[:, start : start + rows], flip, preferred_element_type=jnp.float32)
        total += jnp.dot(
            part.astype(jnp.bfloat16), shifted[:, start : start + count], preferred_element_type=jnp.float32
        )
    return total.astype(jnp.bfloat16)


def first_kernel(line_hbm, bank_hbm, basis_ref, raw_ref, bank_ref, line_ref, sems):
    section = lax.axis_index("sect")
    taps = bank_ref.shape[1]
    wide = basis_ref.shape[1]
    line_copy = pltpu.make_async_copy(line_hbm, raw_ref, sems.at[0])
    bank_copy = pltpu.make_async_copy(bank_hbm, bank_ref, sems.at[1])
    line_copy.start()
    bank_copy.start()
    line_copy.wait()
    line_ref[...] = jnp.zeros_like(line_ref)
    line_ref[0:1, 0 : raw_ref.shape[1]] = raw_ref[...].astype(jnp.float32)
    begin = pl.multiple_of(section * LANES, LANES)
    line = line_ref[0:1, pl.ds(begin, taps + wide)]
    bank_copy.wait()
    basis_ref[...] = convolved(line, bank_ref[...], wide)


def first_columns(line, bank, wide):
    width = line.shape[1] + 1
    return pl.pallas_call(
        first_kernel,
        in_specs=[pl.BlockSpec(memory_space=pltpu.HBM)] * 2,
        out_shape=jax.ShapeDtypeStruct((bank.shape[0], wide), jnp.bfloat16),
        scratch_shapes=[
            pltpu.VMEM(line.shape, line.dtype),
            pltpu.VMEM(bank.shape, bank.dtype),
            pltpu.VMEM((8, width), jnp.float32),
            pltpu.SemaphoreType.DMA((2,)),
        ],
        compiler_params=pltpu.CompilerParams(vmem_limit_bytes=GRANT),
        cost_estimate=pl.CostEstimate(flops=1 << 30, bytes_accessed=1 << 22, transcendentals=0),
        name="first_columns",
    )(pltpu.with_memory_space_constraint(line, pltpu.HBM), pltpu.with_memory_space_constraint(bank, pltpu.HBM))


def last_kernel(own_line_ref, other_line_ref, own_ref, other_ref, first_ref, basis_ref, line_ref):
    section = lax.axis_index("sect")
    taps = own_ref.shape[1]
    share = basis_ref.shape[2]
    length = own_line_ref.shape[1]
    line_ref[...] = jnp.zeros_like(line_ref)
    line_ref[0:1, 0:length] = own_line_ref[...].astype(jnp.float32)
    line_ref[8:9, 0:length] = other_line_ref[...].astype(jnp.float32)
    own = line_ref[0:1, share : share + taps + LANES]
    line = jnp.where(section == 0, line_ref[8:9, 0 : taps + LANES], own)
    bank = jnp.where(section == 0, other_ref[...].astype(jnp.float32), own_ref[...].astype(jnp.float32))
    last = convolved(line, bank.astype(jnp.bfloat16), LANES)
    basis = jnp.concatenate([first_ref[...], last], axis=1)
    for chip in range(basis_ref.shape[0]):
        basis_ref[chip] = basis


def basis_share(own_line, other_line, own, other, first, chips):
    width = own_line.shape[1] + 1
    share = first.shape[1] + LANES
    return pl.pallas_call(
        last_kernel,
        out_shape=jax.ShapeDtypeStruct((chips, own.shape[0], share), jnp.bfloat16),
        scratch_shapes=[pltpu.VMEM((16, width), jnp.float32)],
        compiler_params=pltpu.CompilerParams(vmem_limit_bytes=GRANT),
        name="basis_share",
    )(own_line, other_line, own, other, first)


def split(values):
    high = values.astype(jnp.bfloat16)
    return high, (values - high.astype(jnp.float32)).astype(jnp.bfloat16)


def rows_dot(left, right):
    return lax.dot_general(left, right, (((0,), (0,)), ((), ())), preferred_element_type=jnp.float32)


def wide_kernel(own_ref, basis_ref, kept_ref, sent_ref):
    wide = kept_ref.shape[1]
    value = jnp.dot(own_ref[...], basis_ref[:, 0:wide], preferred_element_type=jnp.float32)
    kept_ref[...] = value
    sent_ref[...] = value.astype(sent_ref.dtype)


def narrow_kernel(own_ref, other_ref, basis_ref, kept_ref, sent_ref):
    section = lax.axis_index("sect")
    wide = basis_ref.shape[1] - LANES

    def multiply(fast_ref):
        value = jnp.dot(fast_ref[...], basis_ref[:, wide:], preferred_element_type=jnp.float32)
        kept_ref[...] = value
        sent_ref[...] = value.astype(sent_ref.dtype)

    @pl.when(section == 0)
    def _():
        multiply(other_ref)

    @pl.when(section == 1)
    def _():
        multiply(own_ref)


def partial_products(kernel, count, *operands):
    columns = operands[0].shape[0]
    return pl.pallas_call(
        kernel,
        out_shape=(
            jax.ShapeDtypeStruct((columns, count), jnp.float32),
            jax.ShapeDtypeStruct((columns, count), SENT),
        ),
        compiler_params=pltpu.CompilerParams(vmem_limit_bytes=GRANT),
        cost_estimate=pl.CostEstimate(flops=1 << 29, bytes_accessed=1 << 21, transcendentals=0),
    )(*operands)


def lags_kernel(series_ref, forward_ref, spectrum_ref, weight_ref):
    length, pieces, lanes = series_ref.shape
    groups = weight_ref.shape[0]
    flat = series_ref.reshape(length * pieces, lanes)

    def part(which):
        halves = [flat[pl.ds(2 * tile + which, length, stride=pieces), :] for tile in range(pieces // 2)]
        return jnp.concatenate(halves, axis=1)

    real_part, imag_part = part(0), part(1)
    high, low = split(real_part * real_part + imag_part * imag_part)
    ones = jnp.ones((length, lanes), jnp.bfloat16)
    weight_ref[...] = rows_dot(high, ones) + rows_dot(low, ones)
    table = forward_ref[0:length, :]
    scale = jnp.float32(1.0 / PERIOD)
    real_hat = rows_dot(real_part.astype(jnp.bfloat16), table) * scale
    imag_hat = rows_dot(imag_part.astype(jnp.bfloat16), table) * scale
    spectrum_ref[0:groups, 0:BINS] = real_hat[:, :BINS] - imag_hat[:, BINS:]
    spectrum_ref[0:groups, BINS:] = real_hat[:, BINS:] + imag_hat[:, :BINS]
    spectrum_ref[groups:, 0:BINS] = real_hat[:, :BINS] + imag_hat[:, BINS:]
    spectrum_ref[groups:, BINS:] = real_hat[:, BINS:] - imag_hat[:, :BINS]


def lag_spectrum(correlation, forward):
    groups, _, length = correlation.shape
    tiles = groups // LANES
    series = correlation.transpose(2, 1, 0).reshape(length, 2, tiles, LANES)
    series = series.transpose(0, 2, 1, 3).reshape(length, 2 * tiles, LANES)
    return pl.pallas_call(
        lags_kernel,
        out_shape=(
            jax.ShapeDtypeStruct((2 * groups, 2 * BINS), jnp.float32),
            jax.ShapeDtypeStruct((groups, LANES), jnp.float32),
        ),
        compiler_params=pltpu.CompilerParams(vmem_limit_bytes=GRANT),
        cost_estimate=pl.CostEstimate(flops=1 << 30, bytes_accessed=1 << 22, transcendentals=0),
        name="lag_spectrum",
    )(series, forward)


def residual_kernel(
    half,
    own_wide_ref,
    own_narrow_ref,
    other_wide_ref,
    other_narrow_ref,
    spectrum_ref,
    weight_ref,
    forward_ref,
    inverse_ref,
    snr_ref,
    residual_ref,
    full_ref,
):
    section = lax.axis_index("sect")
    groups, share = residual_ref.shape
    samples = forward_ref.shape[0]
    length = 2 * half + 1
    tiles = samples // LANES
    lane = lax.broadcasted_iota(jnp.int32, (2 * groups, LANES), 1)

    def placed(slow, middle, left, right):
        for tile in range(tiles):
            start = (tile // 2) * LANES
            picked = slow[:, start : start + LANES].astype(jnp.float32)
            held = jnp.take_along_axis(picked, lane // 2 + (tile % 2) * (LANES // 2), axis=1)
            if tile == 0:
                fast = left[...]
            elif tile == tiles - 1:
                fast = right[...]
            else:
                fast = middle[:, (tile - 1) * LANES : tile * LANES]
            full_ref[tile] = held + fast.astype(jnp.float32)

    @pl.when(section == 0)
    def _():
        placed(own_wide_ref, other_wide_ref, own_narrow_ref, other_narrow_ref)

    @pl.when(section == 1)
    def _():
        placed(other_wide_ref, own_wide_ref, other_narrow_ref, own_narrow_ref)

    first = pl.multiple_of(section * share, share)
    mine = pl.ds(first, share)
    own_tiles = [section * (share // LANES) + step for step in range(share // LANES)]
    even = pl.ds(0, groups, stride=2)
    odd = pl.ds(1, groups, stride=2)

    def joined(rows, which):
        return jnp.concatenate([full_ref[tile, rows, :] for tile in which], axis=1)

    snr_ref[...] = joined(slice(None), own_tiles).astype(jnp.bfloat16)
    real_all = joined(even, range(tiles))
    imag_all = joined(odd, range(tiles))
    real_mid = joined(even, own_tiles)
    imag_mid = joined(odd, own_tiles)
    power = real_all * real_all + imag_all * imag_all
    high, low = split(power)
    source = lax.broadcasted_iota(jnp.int32, (samples, share), 0)
    target = lax.broadcasted_iota(jnp.int32, (samples, share), 1) + first
    band = (jnp.abs(source - target) <= half).astype(jnp.float32).astype(jnp.bfloat16)
    energy = jnp.dot(high, band, preferred_element_type=jnp.float32)
    energy += jnp.dot(low, band, preferred_element_type=jnp.float32)
    table = forward_ref[...]
    real_hat = jnp.dot(real_all.astype(jnp.bfloat16), table, preferred_element_type=jnp.float32)
    imag_hat = jnp.dot(imag_all.astype(jnp.bfloat16), table, preferred_element_type=jnp.float32)
    a_real, a_imag = real_hat[:, :BINS], real_hat[:, BINS:]
    b_real, b_imag = imag_hat[:, :BINS], imag_hat[:, BINS:]
    p_real, p_imag = spectrum_ref[0:groups, 0:BINS], spectrum_ref[0:groups, BINS:]
    q_real, q_imag = spectrum_ref[groups:, 0:BINS], spectrum_ref[groups:, BINS:]
    back = inverse_ref[:, mine]

    def turned(low_part, high_part):
        parts = jnp.concatenate([low_part, high_part], axis=1).astype(jnp.bfloat16)
        return jnp.dot(parts, back, preferred_element_type=jnp.float32)

    up_real, up_imag = a_real - b_imag, a_imag + b_real
    down_real, down_imag = a_real + b_imag, a_imag - b_real
    plus_real = up_real * p_real + up_imag * p_imag
    plus_imag = up_imag * p_real - up_real * p_imag
    minus_real = down_real * q_real + down_imag * q_imag
    minus_imag = down_imag * q_real - down_real * q_imag
    real_sum = turned(plus_real + minus_real, plus_imag + minus_imag)
    imag_sum = turned(plus_imag - minus_imag, minus_real - plus_real)
    cross = real_mid * real_sum + imag_mid * imag_sum
    magnitude = real_mid * real_mid + imag_mid * imag_mid
    weight = jnp.concatenate([weight_ref[...]] * (share // LANES), axis=1)
    residual_ref[...] = (energy - 2.0 * cross + magnitude * weight) * jnp.float32(1.0 / (2.0 * length))


def residual_of(pieces, spectrum, weight, forward, inverse, half, share):
    columns = pieces[0].shape[0]
    return pl.pallas_call(
        functools.partial(residual_kernel, half),
        out_shape=(
            jax.ShapeDtypeStruct((columns, share), jnp.bfloat16),
            jax.ShapeDtypeStruct((columns // 2, share), jnp.float32),
        ),
        scratch_shapes=[pltpu.VMEM((forward.shape[0] // LANES, columns, LANES), jnp.float32)],
        compiler_params=pltpu.CompilerParams(vmem_limit_bytes=GRANT),
        name="residual",
    )(*pieces, spectrum, weight, forward, inverse)


def local(strain, filters, synthesis, correlation):
    sections = lax.axis_size("sect")
    chips = lax.axis_size("tmpl")
    taps = filters.shape[2]
    samples = strain.shape[1] - taps + 1
    half = (correlation.shape[2] - 1) // 2
    share = (samples + samples // 2) // sections
    swap = [(0, 1), (1, 0)]
    forward = jnp.asarray(forward_matrix(samples), jnp.bfloat16)
    inverse = jnp.asarray(inverse_matrix(samples, half), jnp.bfloat16)
    own_bank = filters[0]
    own_rows = synthesis[0]
    other_line = lax.ppermute(strain, "sect", swap)
    other_bank = lax.ppermute(own_bank, "sect", swap)
    other_rows = lax.ppermute(own_rows, "sect", swap)
    first = first_columns(strain, own_bank, share - LANES)
    block = basis_share(strain, other_line, own_bank, other_bank, first, chips)
    mine = lax.all_to_all(block, "tmpl", 0, 0).reshape(-1, share)
    own_wide, sent_wide = partial_products(wide_kernel, share - LANES, own_rows, mine)
    other_wide = lax.ppermute(sent_wide, "sect", swap)
    own_narrow, sent_narrow = partial_products(narrow_kernel, LANES, own_rows, other_rows, mine)
    other_narrow = lax.ppermute(sent_narrow, "sect", swap)
    spectrum, weight = lag_spectrum(correlation, forward)
    pieces = (own_wide, own_narrow, other_wide, other_narrow)
    return residual_of(pieces, spectrum, weight, forward, inverse, half, samples // sections)


def solution(mesh):
    placed = (
        P("sect", None),
        P("sect", "tmpl", None),
        P("sect", "tmpl", None),
        P("tmpl", None, None),
    )
    return jax.shard_map(
        local,
        mesh=mesh,
        in_specs=placed,
        out_specs=(P("tmpl", "sect"), P("tmpl", "sect")),
        check_vma=False,
    )
```

```python
import functools

import jax
import jax.numpy as jnp
import numpy as np
from jax import lax
from jax.experimental import pallas as pl
from jax.experimental.pallas import tpu as pltpu
from jax.sharding import PartitionSpec as P


PERIOD = 767
BINS = 384
LANES = 128
GRANT = 24 << 20
SENT = jnp.float32


def forward_matrix(rows):
    angle = 2.0 * np.pi * np.outer(np.arange(rows), np.arange(BINS)) / PERIOD
    return np.concatenate([np.cos(angle), -np.sin(angle)], axis=1)


def inverse_matrix(samples, half):
    angle = 2.0 * np.pi * np.outer(np.arange(BINS), np.arange(samples) - half) / PERIOD
    share = np.where(np.arange(BINS) == 0, 0.5, 1.0)[:, None]
    return np.concatenate([share * np.cos(angle), -share * np.sin(angle)], axis=0)


def convolved(line, bank, count):
    rows = 256
    taps = bank.shape[1]
    width = line.shape[1]
    row = lax.broadcasted_iota(jnp.int32, (rows, rows), 0)
    col = lax.broadcasted_iota(jnp.int32, (rows, rows), 1)
    flip = (row + col == rows - 1).astype(jnp.float32).astype(jnp.bfloat16)
    spread = jnp.broadcast_to(line, (rows, width))
    shifted = pltpu.roll(spread, width - (rows - 1), 1, stride=1, stride_axis=0).astype(jnp.bfloat16)
    total = jnp.zeros((bank.shape[0], count), jnp.float32)
    starts = range(0, taps, rows)
    stacked = jnp.concatenate([bank[:, start : start + rows] for start in starts], axis=0)
    turned = jnp.dot(stacked, flip, preferred_element_type=jnp.float32).astype(jnp.bfloat16)
    for step, start in enumerate(starts):
        part = turned[step * bank.shape[0] : (step + 1) * bank.shape[0]]
        total += jnp.dot(part, shifted[:, start : start + count], preferred_element_type=jnp.float32)
    return total.astype(jnp.bfloat16)


def first_kernel(line_hbm, bank_hbm, basis_ref, raw_ref, bank_ref, line_ref, sems):
    section = lax.axis_index("sect")
    taps = bank_ref.shape[1]
    wide = basis_ref.shape[1]
    line_copy = pltpu.make_async_copy(line_hbm, raw_ref, sems.at[0])
    bank_copy = pltpu.make_async_copy(bank_hbm, bank_ref, sems.at[1])
    line_copy.start()
    bank_copy.start()
    line_copy.wait()
    line_ref[...] = jnp.zeros_like(line_ref)
    line_ref[0:1, 0 : raw_ref.shape[1]] = raw_ref[...].astype(jnp.float32)
    begin = pl.multiple_of(section * LANES, LANES)
    line = line_ref[0:1, pl.ds(begin, taps + wide)]
    bank_copy.wait()
    basis_ref[...] = convolved(line, bank_ref[...], wide)


def first_columns(line, bank, wide):
    width = line.shape[1] + 1
    return pl.pallas_call(
        first_kernel,
        in_specs=[pl.BlockSpec(memory_space=pltpu.HBM)] * 2,
        out_shape=jax.ShapeDtypeStruct((bank.shape[0], wide), jnp.bfloat16),
        scratch_shapes=[
            pltpu.VMEM(line.shape, line.dtype),
            pltpu.VMEM(bank.shape, bank.dtype),
            pltpu.VMEM((8, width), jnp.float32),
            pltpu.SemaphoreType.DMA((2,)),
        ],
        compiler_params=pltpu.CompilerParams(vmem_limit_bytes=GRANT),
        cost_estimate=pl.CostEstimate(flops=1 << 30, bytes_accessed=1 << 22, transcendentals=0),
        name="first_columns",
    )(pltpu.with_memory_space_constraint(line, pltpu.HBM), pltpu.with_memory_space_constraint(bank, pltpu.HBM))


def last_kernel(own_line_ref, other_line_ref, own_ref, other_ref, first_ref, basis_ref, line_ref):
    section = lax.axis_index("sect")
    taps = own_ref.shape[1]
    share = basis_ref.shape[2]
    length = own_line_ref.shape[1]
    line_ref[...] = jnp.zeros_like(line_ref)
    line_ref[0:1, 0:length] = own_line_ref[...].astype(jnp.float32)
    line_ref[8:9, 0:length] = other_line_ref[...].astype(jnp.float32)
    own = line_ref[0:1, share : share + taps + LANES]
    line = jnp.where(section == 0, line_ref[8:9, 0 : taps + LANES], own)
    bank = jnp.where(section == 0, other_ref[...].astype(jnp.float32), own_ref[...].astype(jnp.float32))
    last = convolved(line, bank.astype(jnp.bfloat16), LANES)
    basis = jnp.concatenate([first_ref[...], last], axis=1)
    for chip in range(basis_ref.shape[0]):
        basis_ref[chip] = basis


def basis_share(own_line, other_line, own, other, first, chips):
    width = own_line.shape[1] + 1
    share = first.shape[1] + LANES
    return pl.pallas_call(
        last_kernel,
        out_shape=jax.ShapeDtypeStruct((chips, own.shape[0], share), jnp.bfloat16),
        scratch_shapes=[pltpu.VMEM((16, width), jnp.float32)],
        compiler_params=pltpu.CompilerParams(vmem_limit_bytes=GRANT),
        name="basis_share",
    )(own_line, other_line, own, other, first)


def split(values):
    high = values.astype(jnp.bfloat16)
    return high, (values - high.astype(jnp.float32)).astype(jnp.bfloat16)


def rows_dot(left, right):
    return lax.dot_general(left, right, (((0,), (0,)), ((), ())), preferred_element_type=jnp.float32)


def wide_kernel(own_ref, basis_ref, kept_ref, sent_ref):
    wide = kept_ref.shape[1]
    value = jnp.dot(own_ref[...], basis_ref[:, 0:wide], preferred_element_type=jnp.float32)
    kept_ref[...] = value
    sent_ref[...] = value.astype(sent_ref.dtype)


def narrow_kernel(own_ref, other_ref, basis_ref, kept_ref, sent_ref):
    section = lax.axis_index("sect")
    wide = basis_ref.shape[1] - LANES

    def multiply(fast_ref):
        value = jnp.dot(fast_ref[...], basis_ref[:, wide:], preferred_element_type=jnp.float32)
        kept_ref[...] = value
        sent_ref[...] = value.astype(sent_ref.dtype)

    @pl.when(section == 0)
    def _():
        multiply(other_ref)

    @pl.when(section == 1)
    def _():
        multiply(own_ref)


def partial_products(kernel, count, *operands):
    columns = operands[0].shape[0]
    return pl.pallas_call(
        kernel,
        out_shape=(
            jax.ShapeDtypeStruct((columns, count), jnp.float32),
            jax.ShapeDtypeStruct((columns, count), SENT),
        ),
        compiler_params=pltpu.CompilerParams(vmem_limit_bytes=GRANT),
        cost_estimate=pl.CostEstimate(flops=1 << 29, bytes_accessed=1 << 21, transcendentals=0),
    )(*operands)


def lags_kernel(series_ref, forward_ref, spectrum_ref, weight_ref):
    length, pieces, lanes = series_ref.shape
    groups = weight_ref.shape[0]
    flat = series_ref.reshape(length * pieces, lanes)

    def part(which):
        halves = [flat[pl.ds(2 * tile + which, length, stride=pieces), :] for tile in range(pieces // 2)]
        return jnp.concatenate(halves, axis=1)

    real_part, imag_part = part(0), part(1)
    high, low = split(real_part * real_part + imag_part * imag_part)
    ones = jnp.ones((length, lanes), jnp.bfloat16)
    weight_ref[...] = rows_dot(high, ones) + rows_dot(low, ones)
    table = forward_ref[0:length, :]
    scale = jnp.float32(1.0 / PERIOD)
    real_hat = rows_dot(real_part.astype(jnp.bfloat16), table) * scale
    imag_hat = rows_dot(imag_part.astype(jnp.bfloat16), table) * scale
    spectrum_ref[0:groups, 0:BINS] = real_hat[:, :BINS] - imag_hat[:, BINS:]
    spectrum_ref[0:groups, BINS:] = real_hat[:, BINS:] + imag_hat[:, :BINS]
    spectrum_ref[groups:, 0:BINS] = real_hat[:, :BINS] + imag_hat[:, BINS:]
    spectrum_ref[groups:, BINS:] = real_hat[:, BINS:] - imag_hat[:, :BINS]


def lag_spectrum(correlation, forward):
    groups, _, length = correlation.shape
    tiles = groups // LANES
    series = correlation.transpose(2, 1, 0).reshape(length, 2, tiles, LANES)
    series = series.transpose(0, 2, 1, 3).reshape(length, 2 * tiles, LANES)
    return pl.pallas_call(
        lags_kernel,
        out_shape=(
            jax.ShapeDtypeStruct((2 * groups, 2 * BINS), jnp.float32),
            jax.ShapeDtypeStruct((groups, LANES), jnp.float32),
        ),
        compiler_params=pltpu.CompilerParams(vmem_limit_bytes=GRANT),
        cost_estimate=pl.CostEstimate(flops=1 << 30, bytes_accessed=1 << 22, transcendentals=0),
        name="lag_spectrum",
    )(series, forward)


def residual_kernel(
    half,
    own_wide_ref,
    own_narrow_ref,
    other_wide_ref,
    other_narrow_ref,
    spectrum_ref,
    weight_ref,
    forward_ref,
    inverse_ref,
    snr_ref,
    residual_ref,
    full_ref,
):
    section = lax.axis_index("sect")
    groups, share = residual_ref.shape
    samples = forward_ref.shape[0]
    length = 2 * half + 1
    tiles = samples // LANES
    lane = lax.broadcasted_iota(jnp.int32, (2 * groups, LANES), 1)

    def placed(slow, middle, left, right):
        for tile in range(tiles):
            start = (tile // 2) * LANES
            picked = slow[:, start : start + LANES].astype(jnp.float32)
            held = jnp.take_along_axis(picked, lane // 2 + (tile % 2) * (LANES // 2), axis=1)
            if tile == 0:
                fast = left[...]
            elif tile == tiles - 1:
                fast = right[...]
            else:
                fast = middle[:, (tile - 1) * LANES : tile * LANES]
            full_ref[tile] = held + fast.astype(jnp.float32)

    @pl.when(section == 0)
    def _():
        placed(own_wide_ref, other_wide_ref, own_narrow_ref, other_narrow_ref)

    @pl.when(section == 1)
    def _():
        placed(other_wide_ref, own_wide_ref, other_narrow_ref, own_narrow_ref)

    first = pl.multiple_of(section * share, share)
    mine = pl.ds(first, share)
    own_tiles = [section * (share // LANES) + step for step in range(share // LANES)]
    even = pl.ds(0, groups, stride=2)
    odd = pl.ds(1, groups, stride=2)

    def joined(rows, which):
        return jnp.concatenate([full_ref[tile, rows, :] for tile in which], axis=1)

    snr_ref[...] = joined(slice(None), own_tiles).astype(jnp.bfloat16)
    real_all = joined(even, range(tiles))
    imag_all = joined(odd, range(tiles))
    real_mid = joined(even, own_tiles)
    imag_mid = joined(odd, own_tiles)
    power = real_all * real_all + imag_all * imag_all
    high, low = split(power)
    source = lax.broadcasted_iota(jnp.int32, (samples, share), 0)
    target = lax.broadcasted_iota(jnp.int32, (samples, share), 1) + first
    band = (jnp.abs(source - target) <= half).astype(jnp.float32).astype(jnp.bfloat16)
    energy = jnp.dot(high, band, preferred_element_type=jnp.float32)
    energy += jnp.dot(low, band, preferred_element_type=jnp.float32)
    table = forward_ref[...]
    real_hat = jnp.dot(real_all.astype(jnp.bfloat16), table, preferred_element_type=jnp.float32)
    imag_hat = jnp.dot(imag_all.astype(jnp.bfloat16), table, preferred_element_type=jnp.float32)
    a_real, a_imag = real_hat[:, :BINS], real_hat[:, BINS:]
    b_real, b_imag = imag_hat[:, :BINS], imag_hat[:, BINS:]
    p_real, p_imag = spectrum_ref[0:groups, 0:BINS], spectrum_ref[0:groups, BINS:]
    q_real, q_imag = spectrum_ref[groups:, 0:BINS], spectrum_ref[groups:, BINS:]
    back = inverse_ref[:, mine]

    def turned(low_part, high_part):
        parts = jnp.concatenate([low_part, high_part], axis=1).astype(jnp.bfloat16)
        return jnp.dot(parts, back, preferred_element_type=jnp.float32)

    up_real, up_imag = a_real - b_imag, a_imag + b_real
    down_real, down_imag = a_real + b_imag, a_imag - b_real
    plus_real = up_real * p_real + up_imag * p_imag
    plus_imag = up_imag * p_real - up_real * p_imag
    minus_real = down_real * q_real + down_imag * q_imag
    minus_imag = down_imag * q_real - down_real * q_imag
    real_sum = turned(plus_real + minus_real, plus_imag + minus_imag)
    imag_sum = turned(plus_imag - minus_imag, minus_real - plus_real)
    cross = real_mid * real_sum + imag_mid * imag_sum
    magnitude = real_mid * real_mid + imag_mid * imag_mid
    weight = jnp.concatenate([weight_ref[...]] * (share // LANES), axis=1)
    residual_ref[...] = (energy - 2.0 * cross + magnitude * weight) * jnp.float32(1.0 / (2.0 * length))


def residual_of(pieces, spectrum, weight, forward, inverse, half, share):
    columns = pieces[0].shape[0]
    return pl.pallas_call(
        functools.partial(residual_kernel, half),
        out_shape=(
            jax.ShapeDtypeStruct((columns, share), jnp.bfloat16),
            jax.ShapeDtypeStruct((columns // 2, share), jnp.float32),
        ),
        scratch_shapes=[pltpu.VMEM((forward.shape[0] // LANES, columns, LANES), jnp.float32)],
        compiler_params=pltpu.CompilerParams(vmem_limit_bytes=GRANT),
        name="residual",
    )(*pieces, spectrum, weight, forward, inverse)


def local(strain, filters, synthesis, correlation):
    sections = lax.axis_size("sect")
    chips = lax.axis_size("tmpl")
    taps = filters.shape[2]
    samples = strain.shape[1] - taps + 1
    half = (correlation.shape[2] - 1) // 2
    share = (samples + samples // 2) // sections
    swap = [(0, 1), (1, 0)]
    forward = jnp.asarray(forward_matrix(samples), jnp.bfloat16)
    inverse = jnp.asarray(inverse_matrix(samples, half), jnp.bfloat16)
    own_bank = filters[0]
    own_rows = synthesis[0]
    other_line = lax.ppermute(strain, "sect", swap)
    other_bank = lax.ppermute(own_bank, "sect", swap)
    other_rows = lax.ppermute(own_rows, "sect", swap)
    first = first_columns(strain, own_bank, share - LANES)
    block = basis_share(strain, other_line, own_bank, other_bank, first, chips)
    mine = lax.all_to_all(block, "tmpl", 0, 0).reshape(-1, share)
    own_wide, sent_wide = partial_products(wide_kernel, share - LANES, own_rows, mine)
    other_wide = lax.ppermute(sent_wide, "sect", swap)
    own_narrow, sent_narrow = partial_products(narrow_kernel, LANES, own_rows, other_rows, mine)
    other_narrow = lax.ppermute(sent_narrow, "sect", swap)
    spectrum, weight = lag_spectrum(correlation, forward)
    pieces = (own_wide, own_narrow, other_wide, other_narrow)
    return residual_of(pieces, spectrum, weight, forward, inverse, half, samples // sections)


def solution(mesh):
    placed = (
        P("sect", None),
        P("sect", "tmpl", None),
        P("sect", "tmpl", None),
        P("tmpl", None, None),
    )
    return jax.shard_map(
        local,
        mesh=mesh,
        in_specs=placed,
        out_specs=(P("tmpl", "sect"), P("tmpl", "sect")),
        check_vma=False,
    )
```

```python
import functools

import jax
import jax.numpy as jnp
import numpy as np
from jax import lax
from jax.experimental import pallas as pl
from jax.experimental.pallas import tpu as pltpu
from jax.sharding import PartitionSpec as P


PERIOD = 767
BINS = 384
LANES = 128
GRANT = 24 << 20


def forward_matrix(rows):
    angle = 2.0 * np.pi * np.outer(np.arange(rows), np.arange(BINS)) / PERIOD
    return np.concatenate([np.cos(angle), -np.sin(angle)], axis=1)


def inverse_matrix(samples, half):
    angle = 2.0 * np.pi * np.outer(np.arange(BINS), np.arange(samples) - half) / PERIOD
    share = np.where(np.arange(BINS) == 0, 0.5, 1.0)[:, None]
    return np.concatenate([share * np.cos(angle), -share * np.sin(angle)], axis=0)


ROWS = 256


def flip_matrix():
    row = lax.broadcasted_iota(jnp.int32, (ROWS, ROWS), 0)
    col = lax.broadcasted_iota(jnp.int32, (ROWS, ROWS), 1)
    return (row + col == ROWS - 1).astype(jnp.float32).astype(jnp.bfloat16)


def toeplitz(line):
    width = line.shape[1]
    spread = jnp.broadcast_to(line, (ROWS, width))
    return pltpu.roll(spread, width - (ROWS - 1), 1, stride=1, stride_axis=0).astype(jnp.bfloat16)


def convolved(shifted, flip, bank, count):
    total = jnp.zeros((bank.shape[0], count), jnp.float32)
    starts = range(0, bank.shape[1], ROWS)
    stacked = jnp.concatenate([bank[:, start : start + ROWS] for start in starts], axis=0)
    turned = jnp.dot(stacked, flip, preferred_element_type=jnp.float32).astype(jnp.bfloat16)
    for step, start in enumerate(starts):
        part = turned[step * bank.shape[0] : (step + 1) * bank.shape[0]]
        total += jnp.dot(part, shifted[:, start : start + count], preferred_element_type=jnp.float32)
    return total.astype(jnp.bfloat16)


def first_kernel(line_hbm, bank_hbm, basis_ref, raw_ref, bank_ref, line_ref, sems):
    section = lax.axis_index("sect")
    taps = bank_ref.shape[1]
    wide = basis_ref.shape[1]
    line_copy = pltpu.make_async_copy(line_hbm, raw_ref, sems.at[0])
    bank_copy = pltpu.make_async_copy(bank_hbm, bank_ref, sems.at[1])
    line_copy.start()
    bank_copy.start()
    line_ref[...] = jnp.zeros_like(line_ref)
    flip = flip_matrix()
    line_copy.wait()
    line_ref[0:1, 0 : raw_ref.shape[1]] = raw_ref[...].astype(jnp.float32)
    begin = pl.multiple_of(section * LANES, LANES)
    bank_copy.wait()
    line = line_ref[0:1, pl.ds(begin, taps + wide)]
    basis_ref[...] = convolved(toeplitz(line), flip, bank_ref[...], wide)


def first_columns(line, bank, wide):
    width = line.shape[1] + 1
    return pl.pallas_call(
        first_kernel,
        in_specs=[pl.BlockSpec(memory_space=pltpu.HBM)] * 2,
        out_shape=jax.ShapeDtypeStruct((bank.shape[0], wide), jnp.bfloat16),
        scratch_shapes=[
            pltpu.VMEM(line.shape, line.dtype),
            pltpu.VMEM(bank.shape, bank.dtype),
            pltpu.VMEM((8, width), jnp.float32),
            pltpu.SemaphoreType.DMA((2,)),
        ],
        compiler_params=pltpu.CompilerParams(vmem_limit_bytes=GRANT),
        cost_estimate=pl.CostEstimate(flops=1 << 30, bytes_accessed=1 << 22, transcendentals=0),
        name="first_columns",
    )(pltpu.with_memory_space_constraint(line, pltpu.HBM), pltpu.with_memory_space_constraint(bank, pltpu.HBM))


def last_kernel(own_line_ref, other_line_ref, own_ref, other_ref, first_ref, basis_ref, line_ref):
    section = lax.axis_index("sect")
    taps = own_ref.shape[1]
    share = basis_ref.shape[2]
    length = own_line_ref.shape[1]
    line_ref[...] = jnp.zeros_like(line_ref)
    line_ref[0:1, 0:length] = own_line_ref[...].astype(jnp.float32)
    line_ref[8:9, 0:length] = other_line_ref[...].astype(jnp.float32)
    own = line_ref[0:1, share : share + taps + LANES]
    line = jnp.where(section == 0, line_ref[8:9, 0 : taps + LANES], own)
    bank = jnp.where(section == 0, other_ref[...].astype(jnp.float32), own_ref[...].astype(jnp.float32))
    last = convolved(toeplitz(line), flip_matrix(), bank.astype(jnp.bfloat16), LANES)
    basis = jnp.concatenate([first_ref[...], last], axis=1)
    for chip in range(basis_ref.shape[0]):
        basis_ref[chip] = basis


def basis_share(own_line, other_line, own, other, first, chips):
    width = own_line.shape[1] + 1
    share = first.shape[1] + LANES
    return pl.pallas_call(
        last_kernel,
        out_shape=jax.ShapeDtypeStruct((chips, own.shape[0], share), jnp.bfloat16),
        scratch_shapes=[pltpu.VMEM((16, width), jnp.float32)],
        compiler_params=pltpu.CompilerParams(vmem_limit_bytes=GRANT),
        name="basis_share",
    )(own_line, other_line, own, other, first)


def split(values):
    high = values.astype(jnp.bfloat16)
    return high, (values - high.astype(jnp.float32)).astype(jnp.bfloat16)


def rows_dot(left, right):
    return lax.dot_general(left, right, (((0,), (0,)), ((), ())), preferred_element_type=jnp.float32)


def wide_kernel(own_ref, basis_ref, part_ref):
    wide = part_ref.shape[1]
    part_ref[...] = jnp.dot(own_ref[...], basis_ref[:, 0:wide], preferred_element_type=jnp.float32)


def narrow_kernel(own_ref, other_ref, basis_ref, part_ref):
    section = lax.axis_index("sect")
    wide = basis_ref.shape[1] - LANES

    def multiply(fast_ref):
        part_ref[...] = jnp.dot(fast_ref[...], basis_ref[:, wide:], preferred_element_type=jnp.float32)

    @pl.when(section == 0)
    def _():
        multiply(other_ref)

    @pl.when(section == 1)
    def _():
        multiply(own_ref)


def partial_products(kernel, count, *operands):
    columns = operands[0].shape[0]
    return pl.pallas_call(
        kernel,
        out_shape=jax.ShapeDtypeStruct((columns, count), jnp.float32),
        compiler_params=pltpu.CompilerParams(vmem_limit_bytes=GRANT),
        cost_estimate=pl.CostEstimate(flops=1 << 29, bytes_accessed=1 << 21, transcendentals=0),
    )(*operands)


def lags_kernel(series_ref, forward_ref, spectrum_ref, weight_ref):
    length, pieces, lanes = series_ref.shape
    groups = weight_ref.shape[0]
    flat = series_ref.reshape(length * pieces, lanes)

    def part(which):
        halves = [flat[pl.ds(2 * tile + which, length, stride=pieces), :] for tile in range(pieces // 2)]
        return jnp.concatenate(halves, axis=1)

    real_part, imag_part = part(0), part(1)
    high, low = split(real_part * real_part + imag_part * imag_part)
    ones = jnp.ones((length, lanes), jnp.bfloat16)
    weight_ref[...] = rows_dot(high, ones) + rows_dot(low, ones)
    table = forward_ref[0:length, :]
    scale = jnp.float32(1.0 / PERIOD)
    real_hat = rows_dot(real_part.astype(jnp.bfloat16), table) * scale
    imag_hat = rows_dot(imag_part.astype(jnp.bfloat16), table) * scale
    spectrum_ref[0:groups, 0:BINS] = real_hat[:, :BINS] - imag_hat[:, BINS:]
    spectrum_ref[0:groups, BINS:] = real_hat[:, BINS:] + imag_hat[:, :BINS]
    spectrum_ref[groups:, 0:BINS] = real_hat[:, :BINS] + imag_hat[:, BINS:]
    spectrum_ref[groups:, BINS:] = real_hat[:, BINS:] - imag_hat[:, :BINS]


def lag_spectrum(correlation, forward):
    groups, _, length = correlation.shape
    tiles = groups // LANES
    series = correlation.transpose(2, 1, 0).reshape(length, 2, tiles, LANES)
    series = series.transpose(0, 2, 1, 3).reshape(length, 2 * tiles, LANES)
    return pl.pallas_call(
        lags_kernel,
        out_shape=(
            jax.ShapeDtypeStruct((2 * groups, 2 * BINS), jnp.float32),
            jax.ShapeDtypeStruct((groups, LANES), jnp.float32),
        ),
        compiler_params=pltpu.CompilerParams(vmem_limit_bytes=GRANT),
        cost_estimate=pl.CostEstimate(flops=1 << 30, bytes_accessed=1 << 22, transcendentals=0),
        name="lag_spectrum",
    )(series, forward)


def residual_kernel(
    half,
    own_wide_ref,
    own_narrow_ref,
    other_wide_ref,
    other_narrow_ref,
    spectrum_ref,
    weight_ref,
    forward_ref,
    inverse_ref,
    snr_ref,
    residual_ref,
    full_ref,
):
    section = lax.axis_index("sect")
    groups, share = residual_ref.shape
    samples = forward_ref.shape[0]
    length = 2 * half + 1
    tiles = samples // LANES
    lane = lax.broadcasted_iota(jnp.int32, (2 * groups, LANES), 1)

    def placed(slow, middle, left, right):
        for tile in range(tiles):
            start = (tile // 2) * LANES
            picked = slow[:, start : start + LANES].astype(jnp.float32)
            held = jnp.take_along_axis(picked, lane // 2 + (tile % 2) * (LANES // 2), axis=1)
            if tile == 0:
                fast = left[...]
            elif tile == tiles - 1:
                fast = right[...]
            else:
                fast = middle[:, (tile - 1) * LANES : tile * LANES]
            full_ref[tile] = held + fast.astype(jnp.float32)

    @pl.when(section == 0)
    def _():
        placed(own_wide_ref, other_wide_ref, own_narrow_ref, other_narrow_ref)

    @pl.when(section == 1)
    def _():
        placed(other_wide_ref, own_wide_ref, other_narrow_ref, own_narrow_ref)

    first = pl.multiple_of(section * share, share)
    mine = pl.ds(first, share)
    own_tiles = [section * (share // LANES) + step for step in range(share // LANES)]
    even = pl.ds(0, groups, stride=2)
    odd = pl.ds(1, groups, stride=2)

    def joined(rows, which):
        return jnp.concatenate([full_ref[tile, rows, :] for tile in which], axis=1)

    snr_ref[...] = joined(slice(None), own_tiles).astype(jnp.bfloat16)
    real_all = joined(even, range(tiles))
    imag_all = joined(odd, range(tiles))
    real_mid = joined(even, own_tiles)
    imag_mid = joined(odd, own_tiles)
    power = real_all * real_all + imag_all * imag_all
    high, low = split(power)
    source = lax.broadcasted_iota(jnp.int32, (samples, share), 0)
    target = lax.broadcasted_iota(jnp.int32, (samples, share), 1) + first
    band = (jnp.abs(source - target) <= half).astype(jnp.float32).astype(jnp.bfloat16)
    energy = jnp.dot(high, band, preferred_element_type=jnp.float32)
    energy += jnp.dot(low, band, preferred_element_type=jnp.float32)
    table = forward_ref[...]
    real_hat = jnp.dot(real_all.astype(jnp.bfloat16), table, preferred_element_type=jnp.float32)
    imag_hat = jnp.dot(imag_all.astype(jnp.bfloat16), table, preferred_element_type=jnp.float32)
    a_real, a_imag = real_hat[:, :BINS], real_hat[:, BINS:]
    b_real, b_imag = imag_hat[:, :BINS], imag_hat[:, BINS:]
    p_real, p_imag = spectrum_ref[0:groups, 0:BINS], spectrum_ref[0:groups, BINS:]
    q_real, q_imag = spectrum_ref[groups:, 0:BINS], spectrum_ref[groups:, BINS:]
    back = inverse_ref[:, mine]

    def turned(low_part, high_part):
        parts = jnp.concatenate([low_part, high_part], axis=1).astype(jnp.bfloat16)
        return jnp.dot(parts, back, preferred_element_type=jnp.float32)

    up_real, up_imag = a_real - b_imag, a_imag + b_real
    down_real, down_imag = a_real + b_imag, a_imag - b_real
    plus_real = up_real * p_real + up_imag * p_imag
    plus_imag = up_imag * p_real - up_real * p_imag
    minus_real = down_real * q_real + down_imag * q_imag
    minus_imag = down_imag * q_real - down_real * q_imag
    real_sum = turned(plus_real + minus_real, plus_imag + minus_imag)
    imag_sum = turned(plus_imag - minus_imag, minus_real - plus_real)
    cross = real_mid * real_sum + imag_mid * imag_sum
    magnitude = real_mid * real_mid + imag_mid * imag_mid
    weight = jnp.concatenate([weight_ref[...]] * (share // LANES), axis=1)
    residual_ref[...] = (energy - 2.0 * cross + magnitude * weight) * jnp.float32(1.0 / (2.0 * length))


def residual_of(pieces, spectrum, weight, forward, inverse, half, share):
    columns = pieces[0].shape[0]
    return pl.pallas_call(
        functools.partial(residual_kernel, half),
        out_shape=(
            jax.ShapeDtypeStruct((columns, share), jnp.bfloat16),
            jax.ShapeDtypeStruct((columns // 2, share), jnp.float32),
        ),
        scratch_shapes=[pltpu.VMEM((forward.shape[0] // LANES, columns, LANES), jnp.float32)],
        compiler_params=pltpu.CompilerParams(vmem_limit_bytes=GRANT),
        name="residual",
    )(*pieces, spectrum, weight, forward, inverse)


def local(strain, filters, synthesis, correlation):
    sections = lax.axis_size("sect")
    chips = lax.axis_size("tmpl")
    taps = filters.shape[2]
    samples = strain.shape[1] - taps + 1
    half = (correlation.shape[2] - 1) // 2
    share = (samples + samples // 2) // sections
    swap = [(0, 1), (1, 0)]
    forward = jnp.asarray(forward_matrix(samples), jnp.bfloat16)
    inverse = jnp.asarray(inverse_matrix(samples, half), jnp.bfloat16)
    own_bank = filters[0]
    own_rows = synthesis[0]
    other_line = lax.ppermute(strain, "sect", swap)
    other_bank = lax.ppermute(own_bank, "sect", swap)
    other_rows = lax.ppermute(own_rows, "sect", swap)
    first = first_columns(strain, own_bank, share - LANES)
    block = basis_share(strain, other_line, own_bank, other_bank, first, chips)
    mine = lax.all_to_all(block, "tmpl", 0, 0).reshape(-1, share)
    own_wide = partial_products(wide_kernel, share - LANES, own_rows, mine)
    other_wide = lax.ppermute(own_wide, "sect", swap)
    own_narrow = partial_products(narrow_kernel, LANES, own_rows, other_rows, mine)
    other_narrow = lax.ppermute(own_narrow, "sect", swap)
    spectrum, weight = lag_spectrum(correlation, forward)
    pieces = (own_wide, own_narrow, other_wide, other_narrow)
    return residual_of(pieces, spectrum, weight, forward, inverse, half, samples // sections)


def solution(mesh):
    placed = (
        P("sect", None),
        P("sect", "tmpl", None),
        P("sect", "tmpl", None),
        P("tmpl", None, None),
    )
    return jax.shard_map(
        local,
        mesh=mesh,
        in_specs=placed,
        out_specs=(P("tmpl", "sect"), P("tmpl", "sect")),
        check_vma=False,
    )
```

```python
import functools

import jax
import jax.numpy as jnp
import numpy as np
from jax import lax
from jax.experimental import pallas as pl
from jax.experimental.pallas import tpu as pltpu
from jax.sharding import PartitionSpec as P


PERIOD = 767
BINS = 384
LANES = 128
GRANT = 24 << 20


def forward_matrix(rows):
    angle = 2.0 * np.pi * np.outer(np.arange(rows), np.arange(BINS)) / PERIOD
    return np.concatenate([np.cos(angle), -np.sin(angle)], axis=1)


def inverse_matrix(samples, half):
    angle = 2.0 * np.pi * np.outer(np.arange(BINS), np.arange(samples) - half) / PERIOD
    share = np.where(np.arange(BINS) == 0, 0.5, 1.0)[:, None]
    return np.concatenate([share * np.cos(angle), -share * np.sin(angle)], axis=0)


ROWS = 256


def flip_matrix():
    row = lax.broadcasted_iota(jnp.int32, (ROWS, ROWS), 0)
    col = lax.broadcasted_iota(jnp.int32, (ROWS, ROWS), 1)
    return (row + col == ROWS - 1).astype(jnp.float32).astype(jnp.bfloat16)


def toeplitz(line):
    width = line.shape[1]
    spread = jnp.broadcast_to(line, (ROWS, width))
    return pltpu.roll(spread, width - (ROWS - 1), 1, stride=1, stride_axis=0).astype(jnp.bfloat16)


def convolved(shifted, flip, bank, count):
    total = jnp.zeros((bank.shape[0], count), jnp.float32)
    starts = range(0, bank.shape[1], ROWS)
    stacked = jnp.concatenate([bank[:, start : start + ROWS] for start in starts], axis=0)
    turned = jnp.dot(stacked, flip, preferred_element_type=jnp.float32).astype(jnp.bfloat16)
    for step, start in enumerate(starts):
        part = turned[step * bank.shape[0] : (step + 1) * bank.shape[0]]
        total += jnp.dot(part, shifted[:, start : start + count], preferred_element_type=jnp.float32)
    return total.astype(jnp.bfloat16)


def first_kernel(line_hbm, bank_hbm, basis_ref, raw_ref, bank_ref, line_ref, sems):
    section = lax.axis_index("sect")
    taps = bank_ref.shape[1]
    wide = basis_ref.shape[1]
    line_copy = pltpu.make_async_copy(line_hbm, raw_ref, sems.at[0])
    bank_copy = pltpu.make_async_copy(bank_hbm, bank_ref, sems.at[1])
    line_copy.start()
    bank_copy.start()
    line_ref[...] = jnp.zeros_like(line_ref)
    flip = flip_matrix()
    line_copy.wait()
    line_ref[0:1, 0 : raw_ref.shape[1]] = raw_ref[...].astype(jnp.float32)
    begin = pl.multiple_of(section * LANES, LANES)
    bank_copy.wait()
    line = line_ref[0:1, pl.ds(begin, taps + wide)]
    basis_ref[...] = convolved(toeplitz(line), flip, bank_ref[...], wide)


def first_columns(line, bank, wide):
    width = line.shape[1] + 1
    return pl.pallas_call(
        first_kernel,
        in_specs=[pl.BlockSpec(memory_space=pltpu.HBM)] * 2,
        out_shape=jax.ShapeDtypeStruct((bank.shape[0], wide), jnp.bfloat16),
        scratch_shapes=[
            pltpu.VMEM(line.shape, line.dtype),
            pltpu.VMEM(bank.shape, bank.dtype),
            pltpu.VMEM((8, width), jnp.float32),
            pltpu.SemaphoreType.DMA((2,)),
        ],
        compiler_params=pltpu.CompilerParams(vmem_limit_bytes=GRANT),
        cost_estimate=pl.CostEstimate(flops=1 << 30, bytes_accessed=1 << 22, transcendentals=0),
        name="first_columns",
    )(pltpu.with_memory_space_constraint(line, pltpu.HBM), pltpu.with_memory_space_constraint(bank, pltpu.HBM))


def last_kernel(own_line_ref, other_line_ref, own_ref, other_ref, first_ref, basis_ref, line_ref):
    section = lax.axis_index("sect")
    taps = own_ref.shape[1]
    share = basis_ref.shape[2]
    length = own_line_ref.shape[1]
    line_ref[...] = jnp.zeros_like(line_ref)
    line_ref[0:1, 0:length] = own_line_ref[...].astype(jnp.float32)
    line_ref[8:9, 0:length] = other_line_ref[...].astype(jnp.float32)
    own = line_ref[0:1, share : share + taps + LANES]
    line = jnp.where(section == 0, line_ref[8:9, 0 : taps + LANES], own)
    bank = jnp.where(section == 0, other_ref[...].astype(jnp.float32), own_ref[...].astype(jnp.float32))
    last = convolved(toeplitz(line), flip_matrix(), bank.astype(jnp.bfloat16), LANES)
    basis = jnp.concatenate([first_ref[...], last], axis=1)
    for chip in range(basis_ref.shape[0]):
        basis_ref[chip] = basis


def basis_share(own_line, other_line, own, other, first, chips):
    width = own_line.shape[1] + 1
    share = first.shape[1] + LANES
    return pl.pallas_call(
        last_kernel,
        out_shape=jax.ShapeDtypeStruct((chips, own.shape[0], share), jnp.bfloat16),
        scratch_shapes=[pltpu.VMEM((16, width), jnp.float32)],
        compiler_params=pltpu.CompilerParams(vmem_limit_bytes=GRANT),
        name="basis_share",
    )(own_line, other_line, own, other, first)


def split(values):
    high = values.astype(jnp.bfloat16)
    return high, (values - high.astype(jnp.float32)).astype(jnp.bfloat16)


def rows_dot(left, right):
    return lax.dot_general(left, right, (((0,), (0,)), ((), ())), preferred_element_type=jnp.float32)


def wide_kernel(own_ref, basis_ref, part_ref):
    wide = part_ref.shape[1]
    part_ref[...] = jnp.dot(own_ref[...], basis_ref[:, 0:wide], preferred_element_type=jnp.float32)


def narrow_kernel(own_ref, other_ref, basis_ref, part_ref):
    section = lax.axis_index("sect")
    wide = basis_ref.shape[1] - LANES

    def multiply(fast_ref):
        part_ref[...] = jnp.dot(fast_ref[...], basis_ref[:, wide:], preferred_element_type=jnp.float32)

    @pl.when(section == 0)
    def _():
        multiply(other_ref)

    @pl.when(section == 1)
    def _():
        multiply(own_ref)


def partial_products(kernel, count, *operands):
    columns = operands[0].shape[0]
    return pl.pallas_call(
        kernel,
        out_shape=jax.ShapeDtypeStruct((columns, count), jnp.float32),
        compiler_params=pltpu.CompilerParams(vmem_limit_bytes=GRANT),
        cost_estimate=pl.CostEstimate(flops=1 << 29, bytes_accessed=1 << 21, transcendentals=0),
    )(*operands)


def lags_kernel(series_ref, forward_ref, inverse_ref, spectrum_ref, weight_ref, back_ref):
    share = back_ref.shape[1]
    back_ref[...] = inverse_ref[:, pl.ds(pl.multiple_of(lax.axis_index("sect") * share, share), share)]
    length, pieces, lanes = series_ref.shape
    groups = weight_ref.shape[0]
    flat = series_ref.reshape(length * pieces, lanes)

    def part(which):
        halves = [flat[pl.ds(2 * tile + which, length, stride=pieces), :] for tile in range(pieces // 2)]
        return jnp.concatenate(halves, axis=1)

    real_part, imag_part = part(0), part(1)
    high, low = split(real_part * real_part + imag_part * imag_part)
    ones = jnp.ones((length, lanes), jnp.bfloat16)
    weight_ref[...] = rows_dot(high, ones) + rows_dot(low, ones)
    table = forward_ref[0:length, :]
    scale = jnp.float32(1.0 / PERIOD)
    real_hat = rows_dot(real_part.astype(jnp.bfloat16), table) * scale
    imag_hat = rows_dot(imag_part.astype(jnp.bfloat16), table) * scale
    spectrum_ref[0:groups, 0:BINS] = real_hat[:, :BINS] - imag_hat[:, BINS:]
    spectrum_ref[0:groups, BINS:] = real_hat[:, BINS:] + imag_hat[:, :BINS]
    spectrum_ref[groups:, 0:BINS] = real_hat[:, :BINS] + imag_hat[:, BINS:]
    spectrum_ref[groups:, BINS:] = real_hat[:, BINS:] - imag_hat[:, :BINS]


def lag_spectrum(correlation, forward, inverse, share):
    groups, _, length = correlation.shape
    tiles = groups // LANES
    series = correlation.transpose(2, 1, 0).reshape(length, 2, tiles, LANES)
    series = series.transpose(0, 2, 1, 3).reshape(length, 2 * tiles, LANES)
    return pl.pallas_call(
        lags_kernel,
        out_shape=(
            jax.ShapeDtypeStruct((2 * groups, 2 * BINS), jnp.float32),
            jax.ShapeDtypeStruct((groups, LANES), jnp.float32),
            jax.ShapeDtypeStruct((2 * BINS, share), jnp.bfloat16),
        ),
        compiler_params=pltpu.CompilerParams(vmem_limit_bytes=GRANT),
        cost_estimate=pl.CostEstimate(flops=1 << 30, bytes_accessed=1 << 22, transcendentals=0),
        name="lag_spectrum",
    )(series, forward, inverse)


def hold_kernel(own_ref, other_ref, held_ref):
    section = lax.axis_index("sect")
    tiles, columns, lanes = held_ref.shape
    lane = lax.broadcasted_iota(jnp.int32, (columns, lanes), 1)

    def placed(slow, middle):
        for tile in range(tiles):
            start = (tile // 2) * lanes
            held = jnp.take_along_axis(slow[:, start : start + lanes], lane // 2 + (tile % 2) * (lanes // 2), axis=1)
            if 0 < tile < tiles - 1:
                held += middle[:, (tile - 1) * lanes : tile * lanes]
            held_ref[tile] = held

    @pl.when(section == 0)
    def _():
        placed(own_ref, other_ref)

    @pl.when(section == 1)
    def _():
        placed(other_ref, own_ref)


def held_tiles(own, other, tiles):
    return pl.pallas_call(
        hold_kernel,
        out_shape=jax.ShapeDtypeStruct((tiles, own.shape[0], LANES), jnp.float32),
        compiler_params=pltpu.CompilerParams(vmem_limit_bytes=GRANT),
        cost_estimate=pl.CostEstimate(flops=1 << 28, bytes_accessed=1 << 21, transcendentals=0),
        name="held_tiles",
    )(own, other)


def residual_kernel(
    half,
    held_ref,
    own_narrow_ref,
    other_narrow_ref,
    spectrum_ref,
    weight_ref,
    forward_ref,
    inverse_ref,
    snr_ref,
    residual_ref,
    full_ref,
):
    section = lax.axis_index("sect")
    groups, share = residual_ref.shape
    samples = forward_ref.shape[0]
    length = 2 * half + 1
    tiles = samples // LANES
    last = tiles - 1
    for tile in range(1, last):
        full_ref[tile] = held_ref[tile]

    def ended(left, right):
        full_ref[0] = held_ref[0] + left[...]
        full_ref[last] = held_ref[last] + right[...]

    @pl.when(section == 0)
    def _():
        ended(own_narrow_ref, other_narrow_ref)

    @pl.when(section == 1)
    def _():
        ended(other_narrow_ref, own_narrow_ref)

    first = pl.multiple_of(section * share, share)
    mine = pl.ds(first, share)
    own_tiles = [section * (share // LANES) + step for step in range(share // LANES)]
    even = pl.ds(0, groups, stride=2)
    odd = pl.ds(1, groups, stride=2)

    def joined(rows, which):
        return jnp.concatenate([full_ref[tile, rows, :] for tile in which], axis=1)

    snr_ref[...] = joined(slice(None), own_tiles).astype(jnp.bfloat16)
    real_all = joined(even, range(tiles))
    imag_all = joined(odd, range(tiles))
    real_mid = joined(even, own_tiles)
    imag_mid = joined(odd, own_tiles)
    power = real_all * real_all + imag_all * imag_all
    high, low = split(power)
    source = lax.broadcasted_iota(jnp.int32, (samples, share), 0)
    target = lax.broadcasted_iota(jnp.int32, (samples, share), 1) + first
    band = (jnp.abs(source - target) <= half).astype(jnp.float32).astype(jnp.bfloat16)
    energy = jnp.dot(high, band, preferred_element_type=jnp.float32)
    energy += jnp.dot(low, band, preferred_element_type=jnp.float32)
    table = forward_ref[...]
    real_hat = jnp.dot(real_all.astype(jnp.bfloat16), table, preferred_element_type=jnp.float32)
    imag_hat = jnp.dot(imag_all.astype(jnp.bfloat16), table, preferred_element_type=jnp.float32)
    a_real, a_imag = real_hat[:, :BINS], real_hat[:, BINS:]
    b_real, b_imag = imag_hat[:, :BINS], imag_hat[:, BINS:]
    p_real, p_imag = spectrum_ref[0:groups, 0:BINS], spectrum_ref[0:groups, BINS:]
    q_real, q_imag = spectrum_ref[groups:, 0:BINS], spectrum_ref[groups:, BINS:]
    back = inverse_ref[...]

    def turned(low_part, high_part):
        parts = jnp.concatenate([low_part, high_part], axis=1).astype(jnp.bfloat16)
        return jnp.dot(parts, back, preferred_element_type=jnp.float32)

    up_real, up_imag = a_real - b_imag, a_imag + b_real
    down_real, down_imag = a_real + b_imag, a_imag - b_real
    plus_real = up_real * p_real + up_imag * p_imag
    plus_imag = up_imag * p_real - up_real * p_imag
    minus_real = down_real * q_real + down_imag * q_imag
    minus_imag = down_imag * q_real - down_real * q_imag
    real_sum = turned(plus_real + minus_real, plus_imag + minus_imag)
    imag_sum = turned(plus_imag - minus_imag, minus_real - plus_real)
    cross = real_mid * real_sum + imag_mid * imag_sum
    magnitude = real_mid * real_mid + imag_mid * imag_mid
    weight = jnp.concatenate([weight_ref[...]] * (share // LANES), axis=1)
    residual_ref[...] = (energy - 2.0 * cross + magnitude * weight) * jnp.float32(1.0 / (2.0 * length))


def residual_of(pieces, spectrum, weight, forward, inverse, half, share):
    columns = pieces[1].shape[0]
    return pl.pallas_call(
        functools.partial(residual_kernel, half),
        out_shape=(
            jax.ShapeDtypeStruct((columns, share), jnp.bfloat16),
            jax.ShapeDtypeStruct((columns // 2, share), jnp.float32),
        ),
        scratch_shapes=[pltpu.VMEM((forward.shape[0] // LANES, columns, LANES), jnp.float32)],
        compiler_params=pltpu.CompilerParams(vmem_limit_bytes=GRANT),
        name="residual",
    )(*pieces, spectrum, weight, forward, inverse)


def local(strain, filters, synthesis, correlation):
    sections = lax.axis_size("sect")
    chips = lax.axis_size("tmpl")
    taps = filters.shape[2]
    samples = strain.shape[1] - taps + 1
    half = (correlation.shape[2] - 1) // 2
    share = (samples + samples // 2) // sections
    swap = [(0, 1), (1, 0)]
    forward = jnp.asarray(forward_matrix(samples), jnp.bfloat16)
    inverse = jnp.asarray(inverse_matrix(samples, half), jnp.bfloat16)
    own_bank = filters[0]
    own_rows = synthesis[0]
    other_line = lax.ppermute(strain, "sect", swap)
    other_bank = lax.ppermute(own_bank, "sect", swap)
    other_rows = lax.ppermute(own_rows, "sect", swap)
    first = first_columns(strain, own_bank, share - LANES)
    block = basis_share(strain, other_line, own_bank, other_bank, first, chips)
    mine = lax.all_to_all(block, "tmpl", 0, 0).reshape(-1, share)
    own_wide = partial_products(wide_kernel, share - LANES, own_rows, mine)
    other_wide = lax.ppermute(own_wide, "sect", swap)
    own_narrow = partial_products(narrow_kernel, LANES, own_rows, other_rows, mine)
    other_narrow = lax.ppermute(own_narrow, "sect", swap)
    spectrum, weight, back = lag_spectrum(correlation, forward, inverse, samples // sections)
    held = held_tiles(own_wide, other_wide, samples // LANES)
    pieces = (held, own_narrow, other_narrow)
    return residual_of(pieces, spectrum, weight, forward, back, half, samples // sections)


def solution(mesh):
    placed = (
        P("sect", None),
        P("sect", "tmpl", None),
        P("sect", "tmpl", None),
        P("tmpl", None, None),
    )
    return jax.shard_map(
        local,
        mesh=mesh,
        in_specs=placed,
        out_specs=(P("tmpl", "sect"), P("tmpl", "sect")),
        check_vma=False,
    )
```
